512 devices in a mesh: fix: 64 (over z, x, core), subj: 8 (over y).
Axes of the slice: x: 4, y: 8, z: 8, core: 2. Of those that a mesh axis runs over, the one named last changes fastest.
Arguments:
- fixels: float32 [65536, 1024], P('fix', 'subj'), may hold values from -6 to 6
- conn_tiles: float32 [512, 4, 128, 128], P('fix'), may hold values from -0.25 to 0.25
- columns: int32 [512, 4], P('fix'), may hold values from 0 to 511, as said below
- nuisance: float32 [4, 1024], P(None, 'subj'), may hold values from -5 to 5
- nuisance_pinv: float32 [4, 1024], P(None, 'subj'), may hold values from -0.1875 to 0.1875
- contrast: float32 [4, 1024], replicated, may hold values from -0.1875 to 0.1875
- perm_table: int32 [128, 1024], P(None, 'subj'), may hold values from 0 to 1023, each once within a row
Outputs:
- projections: float32 [512, 65536], P('subj', 'fix')
The draws below stay inside these ranges and needn't reach their ends.
Inputs may be any that keep to these rules, and one draw needn't show every extreme that they name: `columns`: device j of fix holds blocks j * 8 to (j + 1) * 8 - 1. The 32 entries of one device's rows name blocks of any one device at most 1 times, and in every draw some device's blocks are named exactly 1 times by the rows of every device. `perm_table`: each row is a permutation of the 1024 subjects.
All inputs are finite; a program needn't handle non-finite values.
Results may differ from the reference program's by a relative error of at most 0.000071.
Values sent between devices are 32-bit elements; how exact they have to be, the bound alone decides.
A program may use at most 64 MiB of HBM per device.

```python
import jax
import jax.numpy as jnp
from jax import lax

BS = 128
BLK_DEV = 8
TILES = 4
PERMS = 128
REGS = 4
NUIS = 4
SUBJ = 1024
FIX_BLOCKS = 512
FIXELS = 65536
N_FIX = 64


def draw_columns(key, part):
    hub = jax.random.randint(jax.random.fold_in(key, 7777), (), 0, N_FIX)

    def one_device(device):
        dev_key = jax.random.fold_in(key, device)
        key_order, key_shuffle, key_local = jax.random.split(dev_key, 3)
        order = jax.random.permutation(key_order, N_FIX)
        where_hub = jnp.argmax(order == hub)
        first = order[0]
        order = order.at[where_hub].set(first).at[0].set(hub)
        positions = jnp.arange(BLK_DEV * TILES)
        owners = order[positions % N_FIX]
        owners = jax.random.permutation(key_shuffle, owners)
        local_index = jax.random.randint(key_local, (BLK_DEV * TILES,), 0, BLK_DEV)
        return (owners * BLK_DEV + local_index).reshape(BLK_DEV, TILES)
    result = jax.vmap(one_device)(jnp.arange(N_FIX))
    return result.reshape(N_FIX * BLK_DEV, TILES).astype(jnp.int32)


def level_of(stream_key, shape, cuts, smallest, high):
    factor_of, own = 1.0, jax.random.fold_in(stream_key, 6)
    for dim, shards_of in cuts:
        steps = jnp.exp(jax.random.uniform(jax.random.fold_in(own, dim), (shards_of,), jnp.float32, smallest / len(cuts), high / len(cuts)))
        factor_of = factor_of * jnp.repeat(steps, shape[dim] // shards_of).reshape([-1 if axis == dim else 1 for axis in range(len(shape))])
    return factor_of


def bell_draw(stream_key, shape, scale, most, cuts=(), kind=jnp.bfloat16):
    array = scale * jax.random.normal(stream_key, shape, jnp.float32)
    if cuts:
        array = array * level_of(stream_key, shape, cuts, -0.22, 0.18)
    return jnp.clip(array, -most, most).astype(kind)


def setup_inputs(seed: int = 0) -> dict:
    keys = jax.random.split(jax.random.key(seed), 8)
    fixels = bell_draw(keys[0], (FIXELS, SUBJ), 1.0, 6.0, ((0, 64), (1, 8)), jnp.float32)
    conn_tiles = bell_draw(keys[1], (FIX_BLOCKS, TILES, BS, BS), (BS * TILES) ** -0.5, 0.25, ((0, 64),), jnp.float32)
    columns = draw_columns(jax.random.fold_in(keys[7], 71), 0)
    nuisance = bell_draw(keys[3], (NUIS, SUBJ), 1.0, 5.0, ((1, 8),), jnp.float32)
    nuisance_pinv = bell_draw(keys[4], (NUIS, SUBJ), SUBJ ** -0.5, 0.1875, ((1, 8),), jnp.float32)
    contrast = bell_draw(keys[5], (REGS, SUBJ), SUBJ ** -0.5, 0.1875, (), jnp.float32)
    perm_table = jax.vmap(lambda own: jax.random.permutation(own, SUBJ))(jax.random.split(keys[6], PERMS)).reshape((PERMS, SUBJ)).astype(jnp.int32)
    return dict(fixels=fixels, conn_tiles=conn_tiles, columns=columns, nuisance=nuisance, nuisance_pinv=nuisance_pinv, contrast=contrast, perm_table=perm_table)


def reference(fixels, conn_tiles, columns, nuisance, nuisance_pinv, contrast, perm_table):
    blocks = fixels.reshape(-1, BS, SUBJ)

    def smooth(pieces):
        tile_row, column_row = pieces
        picked = jnp.take(blocks, column_row, axis=0)
        return jnp.einsum("kij,kjs->is", tile_row, picked, precision=lax.Precision.HIGHEST)

    smoothed = lax.map(smooth, (conn_tiles, columns)).reshape(-1, SUBJ)
    fitted = jnp.einsum("ns,fs->nf", nuisance_pinv, smoothed, precision=lax.Precision.HIGHEST)
    residual = smoothed - jnp.einsum("nf,ns->fs", fitted, nuisance, precision=lax.Precision.HIGHEST)
    design = jnp.transpose(jnp.take(contrast, perm_table, axis=1), (1, 0, 2)).reshape(PERMS * REGS, SUBJ)
    return jnp.einsum("cs,fs->cf", design, residual, precision=lax.Precision.HIGHEST)
```

```python
import jax
import jax.numpy as jnp
from jax import lax
from jax.sharding import PartitionSpec as P

HI = lax.Precision.HIGHEST


def design_rows(contrast, perm_table):
    picked = jnp.take(contrast, perm_table, axis=1)
    return jnp.transpose(picked, (1, 0, 2)).reshape(-1, perm_table.shape[1])


def per_device(fixels, conn_tiles, columns, nuisance, nuisance_pinv, contrast, perm_table):
    fix_count = lax.axis_size("fix")
    subj_parts = lax.axis_size("subj")
    block_count, per_row = columns.shape
    block_size = conn_tiles.shape[2]
    nuis = nuisance.shape[0]
    fixel_count = fixels.shape[0]
    tile_total = block_count * per_row
    wanted = columns.reshape(tile_total)
    owners = wanted // block_count
    local_index = wanted % block_count
    capacity = (tile_total + fix_count - 1) // fix_count
    positions = jnp.arange(tile_total)
    earlier = positions[:, None] > positions[None, :]
    same_owner = owners[:, None] == owners[None, :]
    ranks = jnp.sum(jnp.logical_and(same_owner, earlier), axis=1)
    slots = owners * capacity + ranks
    request = jnp.zeros((fix_count * capacity,), jnp.int32).at[slots].set(local_index)
    asked = lax.all_to_all(
        request.reshape(fix_count, capacity), "fix", split_axis=0, concat_axis=0, tiled=True
    ).reshape(-1)
    design = design_rows(contrast, perm_table)
    rows = design.shape[0] // subj_parts
    part = jnp.einsum("cs,fs->cf", design, fixels, precision=HI)
    fit = jnp.einsum("ns,fs->nf", nuisance_pinv, fixels, precision=HI)
    load = jnp.einsum("ns,cs->nc", nuisance, design, precision=HI)
    load = jnp.transpose(load.reshape(nuis, subj_parts, rows), (1, 0, 2))
    load = jnp.pad(load, ((0, 0), (0, 0), (0, fixel_count - rows)))
    fit = jnp.broadcast_to(fit[None], (subj_parts, nuis, fixel_count))
    stacked = jnp.concatenate([part.reshape(subj_parts, rows, fixel_count), fit, load], axis=1)
    summed = lax.psum_scatter(stacked, "subj", scatter_dimension=0, tiled=True)[0]
    own = summed[:rows] - jnp.einsum(
        "nc,nf->cf", summed[rows + nuis :, :rows], summed[rows : rows + nuis], precision=HI
    )
    own_blocks = jnp.transpose(own.reshape(rows, block_count, block_size), (1, 0, 2))
    outgoing = jnp.take(own_blocks, asked, axis=0).reshape(fix_count, capacity, rows, block_size)
    arrived = lax.all_to_all(outgoing, "fix", split_axis=0, concat_axis=0, tiled=True).reshape(
        fix_count * capacity, rows, block_size
    )
    needed = jnp.take(arrived, slots, axis=0).reshape(block_count, per_row, rows, block_size)
    out = jnp.einsum("bkcj,bkij->cbi", needed, conn_tiles, precision=HI)
    return out.reshape(rows, fixel_count)


def solution(mesh):
    placed = (
        P("fix", "subj"),
        P("fix", None, None, None),
        P("fix", None),
        P(None, "subj"),
        P(None, "subj"),
        P(),
        P(None, "subj"),
    )
    return jax.shard_map(
        per_device, mesh=mesh, in_specs=placed, out_specs=P("subj", "fix"), check_vma=False
    )
```

```python
import functools

import jax
import jax.numpy as jnp
from jax import lax
from jax.experimental import pallas as pl
from jax.experimental.pallas import tpu as pltpu
from jax.sharding import PartitionSpec as P

MESH = pl.DeviceIdType.MESH
F32, BF16 = jnp.float32, jnp.bfloat16
BS = 128
NX, NQ = 4, 2
ROWS = 16
EXTRA = 8
NT = (((1,), (1,)), ((), ()))
DIRECT = (2, 3, 6, 7, 1)


def plan(chunks, hy, hz, tiles, rows):
    rate, lat = 46e3, 1.8
    size = rows * BS * 4 * 8
    cost = dict(s0=0.1, a=0.2, fin=0.3, zf=0.05, xp=0.5, xf=0.05, sm=1.2, tp=0.3)
    stages = [("s0", 0)] + [("a", s) for s in range(hy - 1)] + [("fin", 0)]
    stages += [("zf", s) for s in range(hz - 1)] + [("xp", 0), ("xf", 0), ("sm", 0)]
    free = dict(y=0.0, z=0.0, x=0.0)
    at, ready = [0] * chunks, [0.0] * chunks
    order, t, prepared = [], 0.0, 0

    def send(link, amount):
        free[link] = max(free[link], t) + amount / rate
        return free[link] + lat

    while any(i < len(stages) for i in at):
        best, soonest = None, 1e9
        for c in range(chunks):
            if at[c] == len(stages):
                continue
            when = ready[c]
            if at[c] == 0:
                if c and at[c - 1] == 0:
                    continue
                when = max(when, free["y"] - 0.3)
            if stages[at[c]][0] == "sm" and prepared < tiles:
                continue
            if when <= t and best is None:
                best = c
            soonest = min(soonest, when)
        if best is None:
            if prepared < tiles and order:
                order.append(("tp", prepared, 0))
                prepared += 1
                t += cost["tp"]
            else:
                t = max(soonest, t + 1e-6)
            continue
        name, step = stages[at[best]]
        order.append((name, best, step))
        t += cost[name]
        if name == "s0":
            ready[best] = send("y", size / 2)
        elif name == "a":
            ready[best] = send("y", size)
        elif name == "fin":
            ready[best] = send("z", size)
        elif name == "zf":
            ready[best] = send("z", size if step < hz - 2 else size / 2)
        elif name == "xp":
            ready[best] = send("x", size)
            send("x", 2 * size)
        elif name == "xf":
            ready[best] = send("x", size)
        at[best] += 1
    return order


def split3(value, first):
    high = value.astype(BF16)
    low = (value - high.astype(F32)).astype(BF16)
    return [high, high, low] if first else [high, low, high]


def kernel(ny, nz, chunks, *refs):
    (x_ref, t_ref, perm_ref, con_ref, nui_ref, pinv_ref, req_ref, col_ref, out_ref), refs = refs[:9], refs[9:]
    dsc, dcat, xcat, part, gpart, mts, gfin, mcol, tv, thi, tlo, rq, rqs = refs[:13]
    refs = refs[13:]
    sb, refs = refs[:chunks], refs[chunks:]
    rb, refs = refs[:chunks], refs[chunks:]
    zb, refs = refs[:chunks], refs[chunks:]
    pk, refs = refs[:chunks], refs[chunks:]
    xr, refs = refs[:chunks], refs[chunks:]
    rl, refs = refs[:chunks], refs[chunks:]
    ys, yr, zs, zr, xs, xv, fs, fv, hs, hv, qs, qv, loc = refs
    hy, hz = ny // 2, nz // 2
    blocks = x_ref.shape[0] // BS
    half = blocks // 2
    zh = nz // 2
    rows = ROWS
    per_dest = rows * chunks
    perms = perm_ref.shape[0]
    regs = con_ref.shape[0]
    nuis = nui_ref.shape[0]
    cdim = perms * regs

    fix, y = lax.axis_index("fix"), lax.axis_index("subj")
    q = lax.rem(fix, NQ)
    x = lax.rem(fix // NQ, NX)
    z = fix // (NQ * NX)
    m = x * NQ + q

    def fix_of(zz, xx, qq):
        return (zz * NX + xx) * NQ + qq

    x_by = {0: x, 1: x + 1 - 2 * lax.rem(x, 2), 2: lax.rem(x + 2, NX), 3: NX - 1 - x}
    q_by = {0: q, 1: 1 - q}
    y_to = [lax.rem(y + 1, ny), lax.rem(y + ny - 1, ny)]
    z_to = [lax.rem(z + 1, nz), lax.rem(z + nz - 1, nz)]

    def y_dev(d):
        return (fix, y_to[d])

    def z_dev(d):
        return (fix_of(z_to[d], x, q), y)

    def x_dev(o):
        return (fix_of(z, x_by[o // 2], q_by[o % 2]), y)

    def x_slot(o):
        return x_by[o // 2] * NQ + q_by[o % 2]

    peers = [y_dev(0), y_dev(1), z_dev(0), z_dev(1)] + [x_dev(o) for o in range(1, 8)]
    barrier = pltpu.get_barrier_semaphore()
    for peer in peers:
        pl.semaphore_signal(barrier, inc=1, device_id=peer, device_id_type=MESH)

    tile_copy = pltpu.make_async_copy(t_ref, tv, loc.at[0])
    tile_copy.start()
    sent = []

    def remote(src, dst, send_sem, recv_sem, device):
        copy = pltpu.make_async_remote_copy(
            src_ref=src, dst_ref=dst, send_sem=send_sem, recv_sem=recv_sem,
            device_id=device, device_id_type=MESH,
        )
        copy.start()
        sent.append(copy)
        return copy

    index = perm_ref[...]
    group, lane = index // BS, lax.rem(index, BS)
    for r in range(regs):
        picked = jnp.zeros((perms, BS), F32)
        for g in range(con_ref.shape[1] // BS):
            table = jnp.broadcast_to(con_ref[r : r + 1, g * BS : (g + 1) * BS], (perms, BS))
            value = jnp.take_along_axis(table, lane, axis=1, mode="promise_in_bounds")
            picked = jnp.where(group == g, value, picked)
        dsc[pl.ds(r, perms, stride=regs), :] = picked
    for i, piece in enumerate(split3(dsc[...], True)):
        dcat[0:cdim, i * BS : (i + 1) * BS] = piece
    pinv = jnp.concatenate([pinv_ref[...], jnp.zeros((16 - nuis, BS), F32)], axis=0)
    for i, piece in enumerate(split3(pinv, True)):
        dcat[cdim : cdim + 16, i * BS : (i + 1) * BS] = piece
    for i, piece in enumerate(split3(x_ref[...], False)):
        xcat[:, i * BS : (i + 1) * BS] = piece
    nui = jnp.concatenate([jnp.zeros((nuis, BS), F32), nui_ref[...], jnp.zeros((16 - 2 * nuis, BS), F32)], axis=0)
    ncat = jnp.concatenate(split3(nui, False), axis=1)
    load = lax.dot_general(ncat, dcat[0:cdim, :], NT, preferred_element_type=F32)
    for i in range(cdim // BS):
        mts[i] = load[0:EXTRA, i * BS : (i + 1) * BS]
    for b in range(0, blocks, 2):
        both = lax.dot_general(dcat[...], xcat[b * BS : (b + 2) * BS, :], NT, preferred_element_type=F32)
        for i in range(2):
            mine = both[:, i * BS : (i + 1) * BS]
            part[:, b + i] = mine[0:cdim].reshape(ny, per_dest, BS)
            gpart[b + i] = mine[cdim : cdim + EXTRA]

    def store_own(ref, dest, c, lo, hi, add):
        top = part[dest, lo:hi, c * rows : (c + 1) * rows, :]
        ref[lo:hi, 0:rows, :] = ref[lo:hi, 0:rows, :] + top if add else top
        if c == 0:
            more = gpart[lo:hi]
            ref[lo:hi, rows : rows + EXTRA, :] = ref[lo:hi, rows : rows + EXTRA, :] + more if add else more
            if lo == 0:
                per = BS // per_dest
                ref[0, rows : rows + EXTRA, :] = ref[0, rows : rows + EXTRA, :] + mts[dest // per]

    pl.semaphore_wait(barrier, len(peers))

    rq[m] = req_ref[...]
    asks = [remote(req_ref, rq.at[m], qs.at[o], qv.at[o], x_dev(o)) for o in range(1, 8)]
    flights = {}

    def step_s0(c, _):
        store_own(sb[c], lax.rem(y + hy, ny), c, 0, blocks, False)
        flights["y", c, 0, 0] = remote(
            sb[c].at[0:half], rb[c].at[0, 0, 0:half], ys.at[c, 0, 0], yr.at[c, 0, 0], y_dev(0))
        flights["y", c, 0, 1] = remote(
            sb[c].at[half:blocks], rb[c].at[1, 0, half:blocks], ys.at[c, 0, 1], yr.at[c, 0, 1], y_dev(1))

    def step_a(c, s):
        for d in range(2):
            flights["y", c, s, d].wait_recv()
            far = hy - 1 - s
            dest = lax.rem(y + (far if d == 0 else ny - far), ny)
            held = rb[c].at[d, s]
            if s == 0:
                lo, hi = (0, half) if d == 0 else (half, blocks)
                store_own(held, dest, c, lo, hi, True)
                other = (half, blocks) if d == 0 else (0, half)
                store_own(held, dest, c, other[0], other[1], False)
            else:
                store_own(held, dest, c, 0, blocks, True)
            flights["y", c, s + 1, d] = remote(
                held, rb[c].at[d, s + 1], ys.at[c, s + 1, d], yr.at[c, s + 1, d], y_dev(d))

    def z_send(c, s, d):
        src = lax.rem(z + (nz - s if d == 0 else s), nz)
        ref = zb[c].at[src]
        if s == hz - 1:
            ref = zb[c].at[src, 0:half] if d == 0 else zb[c].at[src, half:blocks]
        flights["z", c, s, d] = remote(ref, ref, zs.at[c, s, d], zr.at[c, s, d], z_dev(d))

    def step_fin(c, _):
        for d in range(2):
            flights["y", c, hy - 1, d].wait_recv()
        held = rb[c].at[0, hy - 1]
        store_own(held, y, c, 0, blocks, True)
        if c == 0:
            more = held[:, rows : rows + EXTRA, :] + rb[c][1, hy - 1, :, rows : rows + EXTRA, :]
            gfin[...] = more
            square = jnp.concatenate([more[0], jnp.zeros((BS - EXTRA, BS), F32)], axis=0)
            mcol[...] = jnp.transpose(square)
        total = held[:, 0:rows, :] + rb[c][1, hy - 1, :, 0:rows, :]
        per = BS // per_dest
        cols = mcol[pl.ds(lax.rem(y, per) * per_dest + c * rows, rows), :]
        for n in range(nuis):
            weight = jnp.broadcast_to(cols[:, nuis + n : nuis + n + 1], (rows, BS))
            total = total - weight[None] * gfin[:, n : n + 1, :]
        zb[c][z] = total
        for d in range(2):
            z_send(c, 0, d)

    def step_zf(c, s):
        for d in range(2):
            flights["z", c, s, d].wait_recv()
            z_send(c, s + 1, d)

    ready_asks = []

    def step_xp(c, _):
        if not ready_asks:
            for ask in asks:
                ask.wait_recv()
            copy = pltpu.make_async_copy(rq, rqs, loc.at[1])
            copy.start()
            copy.wait()
            ready_asks.append(1)
        for d in range(2):
            flights["z", c, hz - 1, d].wait_recv()
        for o in (4, 5) + DIRECT:
            e = x_slot(o)
            for zz in range(nz):
                pk[c][o, zz] = zb[c][zz, rqs[e, zz, m]]
            if o in (4, 5):
                for way in range(2):
                    flights["h", c, way, o - 4] = remote(
                        pk[c].at[o, way * zh : (way + 1) * zh], rl[c].at[way, o - 4],
                        hs.at[c, way, o - 4], hv.at[c, way, o - 4], x_dev(2 if way == 0 else 6))
            else:
                flights["x", c, o] = remote(pk[c].at[o], xr[c].at[m], xs.at[c, o], xv.at[c, o], x_dev(o))
        for zz in range(nz):
            xr[c][m, zz] = zb[c][zz, rqs[m, zz, m]]

    def step_xf(c, _):
        for way in range(2):
            for b in range(2):
                flights["h", c, way, b].wait_recv()
                source = x_slot(2 if way == 0 else 6)
                flights["f", c, way, b] = remote(
                    rl[c].at[way, b], xr[c].at[source, way * zh : (way + 1) * zh],
                    fs.at[c, way, b], fv.at[c, way, b], x_dev((6 if way == 0 else 2) + b))

    def step_tp(b, _):
        if b == 0:
            tile_copy.wait()
        for k in range(tv.shape[1]):
            tile = tv[b, k]
            high = tile.astype(BF16)
            thi[b, :, k * BS : (k + 1) * BS] = high
            tlo[b, :, k * BS : (k + 1) * BS] = (tile - high.astype(F32)).astype(BF16)

    def step_sm(c, _):
        for o in DIRECT:
            flights["x", c, o].wait_recv()
        for way in range(2):
            for b in range(2):
                flights["f", c, way, b].wait_recv()
        for b in range(blocks):
            pieces = []
            for k in range(tv.shape[1]):
                col = col_ref[b, k]
                owner = col // blocks
                pieces.append(xr[c][lax.rem(owner, NX * NQ), owner // (NX * NQ)])
            value = jnp.concatenate(pieces, axis=1)
            high = value.astype(BF16).astype(F32)
            both = jnp.concatenate([high, value - high], axis=0).astype(BF16)
            first = lax.dot_general(both, thi[b], NT, preferred_element_type=F32)
            second = lax.dot_general(both, tlo[b], NT, preferred_element_type=F32)
            out_ref[c * rows : (c + 1) * rows, b * BS : (b + 1) * BS] = (
                first[0:rows] + (first[rows:] + second[0:rows]))

    steps = dict(s0=step_s0, a=step_a, fin=step_fin, zf=step_zf, xp=step_xp, xf=step_xf, tp=step_tp, sm=step_sm)
    for name, which, step in plan(chunks, hy, hz, blocks, rows):
        steps[name](which, step)
    for copy in sent:
        copy.wait_send()


def per_device(fixels, conn_tiles, columns, nuisance, nuisance_pinv, contrast, perm_table):
    ny = lax.axis_size("subj")
    nz = lax.axis_size("fix") // (NX * NQ)
    blocks, tiles = columns.shape
    fixel_count = fixels.shape[0]
    perms, regs = perm_table.shape[0], contrast.shape[0]
    cdim = perms * regs
    per_dest = cdim // ny
    chunks = per_dest // ROWS
    wanted = columns.reshape(1, 1, -1)
    group = NX * NQ
    line = lax.broadcasted_iota(jnp.int32, (nz, BS, 1), 0)
    lane = lax.broadcasted_iota(jnp.int32, (nz, BS, 1), 1)
    hit = jnp.logical_and(wanted // blocks == line * group + lane, lane < group)
    request = jnp.sum(jnp.where(hit, wanted % blocks, 0), axis=2)
    vm = pltpu.VMEM
    rc = [ROWS + (EXTRA if c == 0 else 0) for c in range(chunks)]
    hy, hz = ny // 2, nz // 2
    sem = pltpu.SemaphoreType.DMA
    scratch = [
        vm((cdim, BS), F32), vm((cdim + 16, 3 * BS), BF16), vm((fixel_count, 3 * BS), BF16),
        vm((ny, blocks, per_dest, BS), F32), vm((blocks, EXTRA, BS), F32), vm((cdim // BS, EXTRA, BS), F32),
        vm((blocks, EXTRA, BS), F32), vm((BS, BS), F32),
        vm(conn_tiles.shape, F32), vm((blocks, BS, tiles * BS), BF16), vm((blocks, BS, tiles * BS), BF16),
        vm((group, nz, BS), jnp.int32), pltpu.SMEM((group, nz, BS), jnp.int32),
    ]
    scratch += [vm((blocks, r, BS), F32) for r in rc]
    scratch += [vm((2, hy, blocks, r, BS), F32) for r in rc]
    scratch += [vm((nz, blocks, ROWS, BS), F32) for _ in rc]
    scratch += [vm((group, nz, ROWS, BS), F32) for _ in rc]
    scratch += [vm((group, nz, ROWS, BS), F32) for _ in rc]
    scratch += [vm((2, 2, nz // 2, ROWS, BS), F32) for _ in rc]
    scratch += [
        sem((chunks, hy, 2)), sem((chunks, hy, 2)), sem((chunks, hz, 2)), sem((chunks, hz, 2)),
        sem((chunks, 8)), sem((chunks, 8)), sem((chunks, 2, 2)), sem((chunks, 2, 2)),
        sem((chunks, 2, 2)), sem((chunks, 2, 2)), sem((8,)), sem((8,)), sem((2,)),
    ]
    spec = pl.BlockSpec(memory_space=pltpu.VMEM)
    return pl.pallas_call(
        functools.partial(kernel, ny, nz, chunks),
        out_shape=jax.ShapeDtypeStruct((per_dest, fixel_count), F32),
        in_specs=[spec, pl.BlockSpec(memory_space=pl.ANY), spec, spec, spec, spec, spec,
                  pl.BlockSpec(memory_space=pltpu.SMEM)],
        out_specs=spec,
        scratch_shapes=scratch,
        compiler_params=pltpu.CompilerParams(collective_id=0, has_side_effects=True),
        name="project_exchange",
    )(fixels, conn_tiles, perm_table, contrast, nuisance, nuisance_pinv, request, columns)


def solution(mesh):
    placed = (
        P("fix", "subj"),
        P("fix", None, None, None),
        P("fix", None),
        P(None, "subj"),
        P(None, "subj"),
        P(),
        P(None, "subj"),
    )
    return jax.shard_map(
        per_device, mesh=mesh, in_specs=placed, out_specs=P("subj", "fix"), check_vma=False
    )
```

```python
import functools

import jax
import jax.numpy as jnp
from jax import lax
from jax.experimental import pallas as pl
from jax.experimental.pallas import tpu as pltpu
from jax.sharding import PartitionSpec as P

MESH = pl.DeviceIdType.MESH
F32, BF16 = jnp.float32, jnp.bfloat16
BS = 128
NX, NQ = 4, 2
ROWS = 8
WINDOW = 4
RATE, LATENCY = 50e3, 1.8
EXTRA = 8
NT = (((1,), (1,)), ((), ()))
PARTNERS = (4, 5, 2, 3, 6, 7, 1)


def plan(chunks, hy, hz, tiles, rows):
    rate, lat = RATE, LATENCY
    size = rows * BS * 4 * 8
    cost = dict(s0=0.1, a=0.2, fin=0.3, zf=0.05, xp=0.5, sm=1.2, tp=0.3)
    stages = [("s0", 0)] + [("a", s) for s in range(hy - 1)] + [("fin", 0)]
    stages += [("zf", s) for s in range(hz - 1)] + [("xp", 0), ("sm", 0)]
    free = dict(y=0.0, z=0.0, x=0.0)
    at, ready = [0] * chunks, [0.0] * chunks
    order, t, prepared = [], 0.0, 0

    def send(link, amount):
        free[link] = max(free[link], t) + amount / rate
        return free[link] + lat

    while any(i < len(stages) for i in at):
        best, late, soonest = None, None, 1e9
        for c in range(chunks):
            if at[c] == len(stages):
                continue
            when = ready[c]
            if at[c] == 0:
                if c and at[c - 1] == 0:
                    continue
                if sum(0 < i <= hy for i in at) >= WINDOW:
                    continue
                when = max(when, free["y"] - 0.3)
            if stages[at[c]][0] == "sm":
                if prepared < tiles:
                    continue
                if when <= t and late is None:
                    late = c
            elif when <= t and best is None:
                best = c
            soonest = min(soonest, when)
        best = late if best is None else best
        if best is None:
            if prepared < tiles and order:
                order.append(("tp", prepared, 0))
                prepared += 1
                t += cost["tp"]
            else:
                t = max(soonest, t + 1e-6)
            continue
        name, step = stages[at[best]]
        order.append((name, best, step))
        t += cost[name]
        if name == "s0":
            ready[best] = send("y", size / 2)
        elif name == "a":
            ready[best] = send("y", size)
        elif name == "fin":
            ready[best] = send("z", size)
        elif name == "zf":
            ready[best] = send("z", size if step < hz - 2 else size / 2)
        elif name == "xp":
            ready[best] = send("x", 4 * size) + 0.7
        at[best] += 1
    return order


def split3(value, first):
    high = value.astype(BF16)
    low = (value - high.astype(F32)).astype(BF16)
    return [high, high, low] if first else [high, low, high]


def kernel(ny, nz, chunks, *refs):
    (x_hbm, t_ref, perm_hbm, con_hbm, nui_hbm, pinv_hbm, col_hbm, out_ref), refs = refs[:8], refs[8:]
    (x_ref, perm_ref, con_ref, nui_ref, pinv_ref, req_ref, col_ref), refs = refs[:7], refs[7:]
    dsc, dcat, xcat, part, gpart, mts, gfin, mcol, tv, thi, tlo, rq, rqs = refs[:13]
    refs = refs[13:]
    sb, refs = refs[:chunks], refs[chunks:]
    rb, refs = refs[:chunks], refs[chunks:]
    zb, refs = refs[:chunks], refs[chunks:]
    pk, refs = refs[:chunks], refs[chunks:]
    xr, refs = refs[:chunks], refs[chunks:]
    ys, yr, zr, xv, one, loc = refs
    hy, hz = ny // 2, nz // 2
    blocks = x_ref.shape[0] // BS
    half = blocks // 2
    rows = ROWS
    per_dest = rows * chunks
    perms = perm_ref.shape[0]
    regs = con_ref.shape[0]
    nuis = nui_ref.shape[0]
    cdim = perms * regs

    fix, y = lax.axis_index("fix"), lax.axis_index("subj")
    q = lax.rem(fix, NQ)
    x = lax.rem(fix // NQ, NX)
    z = fix // (NQ * NX)
    m = x * NQ + q

    def fix_of(zz, xx, qq):
        return (zz * NX + xx) * NQ + qq

    x_by = {0: x, 1: x + 1 - 2 * lax.rem(x, 2), 2: lax.rem(x + 2, NX), 3: NX - 1 - x}
    q_by = {0: q, 1: 1 - q}
    y_to = [lax.rem(y + 1, ny), lax.rem(y + ny - 1, ny)]
    z_to = [lax.rem(z + 1, nz), lax.rem(z + nz - 1, nz)]

    def y_dev(d):
        return (fix, y_to[d])

    def z_dev(d):
        return (fix_of(z_to[d], x, q), y)

    def x_dev(o):
        return (fix_of(z, x_by[o // 2], q_by[o % 2]), y)

    def x_slot(o):
        return x_by[o // 2] * NQ + q_by[o % 2]

    peers = [y_dev(0), y_dev(1), z_dev(0), z_dev(1)] + [x_dev(o) for o in range(1, 8)]
    barrier = pltpu.get_barrier_semaphore()
    for peer in peers:
        pl.semaphore_signal(barrier, inc=1, device_id=peer, device_id_type=MESH)

    loads = []
    for i, (src, dst) in enumerate((
        (perm_hbm, perm_ref), (con_hbm, con_ref), (x_hbm, x_ref), (nui_hbm, nui_ref),
        (pinv_hbm, pinv_ref), (col_hbm, col_ref), (t_ref, tv),
    )):
        loads.append(pltpu.make_async_copy(src, dst, loc.at[i]))
        loads[-1].start()

    def arrived(ref, sem):
        pltpu.make_async_copy(ref, ref, sem).wait()

    def remote(src, dst, send_sem, recv_sem, device):
        copy = pltpu.make_async_remote_copy(
            src_ref=src, dst_ref=dst, send_sem=send_sem, recv_sem=recv_sem,
            device_id=device, device_id_type=MESH,
        )
        copy.start()

    loads[0].wait()
    loads[1].wait()
    index = perm_ref[...]
    group, lane = index // BS, lax.rem(index, BS)
    for r in range(regs):
        picked = jnp.zeros((perms, BS), F32)
        for g in range(con_ref.shape[1] // BS):
            table = jnp.broadcast_to(con_ref[r : r + 1, g * BS : (g + 1) * BS], (perms, BS))
            value = jnp.take_along_axis(table, lane, axis=1, mode="promise_in_bounds")
            picked = jnp.where(group == g, value, picked)
        dsc[pl.ds(r, perms, stride=regs), :] = picked
    for i, piece in enumerate(split3(dsc[...], True)):
        dcat[0:cdim, i * BS : (i + 1) * BS] = piece
    for i in range(2, 6):
        loads[i].wait()
    pinv = jnp.concatenate([pinv_ref[...], jnp.zeros((16 - nuis, BS), F32)], axis=0)
    for i, piece in enumerate(split3(pinv, True)):
        dcat[cdim : cdim + 16, i * BS : (i + 1) * BS] = piece
    for i, piece in enumerate(split3(x_ref[...], False)):
        xcat[:, i * BS : (i + 1) * BS] = piece
    nui = jnp.concatenate([jnp.zeros((nuis, BS), F32), nui_ref[...], jnp.zeros((16 - 2 * nuis, BS), F32)], axis=0)
    ncat = jnp.concatenate(split3(nui, False), axis=1)
    load = lax.dot_general(ncat, dcat[0:cdim, :], NT, preferred_element_type=F32)
    for i in range(cdim // BS):
        mts[i] = load[0:EXTRA, i * BS : (i + 1) * BS]
    for b in range(0, blocks, 2):
        both = lax.dot_general(dcat[...], xcat[b * BS : (b + 2) * BS, :], NT, preferred_element_type=F32)
        for i in range(2):
            mine = both[:, i * BS : (i + 1) * BS]
            part[:, b + i] = mine[0:cdim].reshape(ny, per_dest, BS)
            gpart[b + i] = mine[cdim : cdim + EXTRA]

    def store_own(ref, dest, c, lo, hi, add):
        top = part[dest, lo:hi, c * rows : (c + 1) * rows, :]
        ref[lo:hi, 0:rows, :] = ref[lo:hi, 0:rows, :] + top if add else top
        if c == 0:
            more = gpart[lo:hi]
            ref[lo:hi, rows : rows + EXTRA, :] = ref[lo:hi, rows : rows + EXTRA, :] + more if add else more
            if lo == 0:
                per = BS // per_dest
                ref[0, rows : rows + EXTRA, :] = ref[0, rows : rows + EXTRA, :] + mts[dest // per]

    line = lax.broadcasted_iota(jnp.int32, (nz, BS), 0)
    place = lax.broadcasted_iota(jnp.int32, (nz, BS), 1)
    place = jnp.where(place < NX * NQ, line * (NX * NQ) + place, -1)
    request = jnp.zeros((nz, BS), jnp.int32)
    for b in range(blocks):
        for k in range(tv.shape[1]):
            col = col_ref[k, b]
            request = jnp.where(place == col // blocks, lax.rem(col, blocks), request)
    req_ref[...] = request
    rq[m] = request

    pl.semaphore_wait(barrier, len(peers))

    def step_s0(c, _):
        store_own(sb[c], lax.rem(y + hy, ny), c, 0, blocks, False)
        out = ys.at[min(c, 1)]
        remote(sb[c].at[0:half], rb[c].at[0, 0:half], out, yr.at[c, 0], y_dev(0))
        remote(sb[c].at[half:blocks], rb[c].at[1, half:blocks], out, yr.at[c, 0], y_dev(1))
        if c == 0:
            for o in range(1, 8):
                remote(req_ref, rq.at[m], one.at[2], one.at[3], x_dev(o))

    def step_a(c, s):
        arrived(rb[c].at[0] if s == 0 else rb[c].at[0:2], yr.at[c, s % 2])
        for d in range(2):
            far = hy - 1 - s
            dest = lax.rem(y + (far if d == 0 else ny - far), ny)
            held = rb[c].at[2 * s + d]
            if s == 0:
                lo, hi = (0, half) if d == 0 else (half, blocks)
                store_own(held, dest, c, lo, hi, True)
                other = (half, blocks) if d == 0 else (0, half)
                store_own(held, dest, c, other[0], other[1], False)
            else:
                store_own(held, dest, c, 0, blocks, True)
            remote(held, rb[c].at[2 * s + 2 + d], ys.at[min(c, 1)], yr.at[c, (s + 1) % 2], y_dev(d))

    def z_send(c, s, d):
        src = lax.rem(z + (nz - s if d == 0 else s), nz)
        ref = zb[c].at[src]
        if s == hz - 1:
            ref = zb[c].at[src, 0:half] if d == 0 else zb[c].at[src, half:blocks]
        remote(ref, ref, one.at[0], zr.at[c, s % 2], z_dev(d))

    def step_fin(c, _):
        arrived(rb[c].at[0:2], yr.at[c, (hy - 1) % 2])
        held = rb[c].at[2 * hy - 2]
        store_own(held, y, c, 0, blocks, True)
        if c == 0:
            more = held[:, rows : rows + EXTRA, :] + rb[c][2 * hy - 1, :, rows : rows + EXTRA, :]
            gfin[...] = more
            square = jnp.concatenate([more[0], jnp.zeros((BS - EXTRA, BS), F32)], axis=0)
            mcol[...] = jnp.transpose(square)
        total = held[:, 0:rows, :] + rb[c][2 * hy - 1, :, 0:rows, :]
        per = BS // per_dest
        cols = mcol[pl.ds(lax.rem(y, per) * per_dest + c * rows, rows), :]
        for n in range(nuis):
            weight = jnp.broadcast_to(cols[:, nuis + n : nuis + n + 1], (rows, BS))
            total = total - weight[None] * gfin[:, n : n + 1, :]
        zb[c][z] = total
        for d in range(2):
            z_send(c, 0, d)

    def step_zf(c, s):
        arrived(zb[c].at[0:2], zr.at[c, s % 2])
        for d in range(2):
            z_send(c, s + 1, d)

    ready_asks = []

    def step_xp(c, _):
        if not ready_asks:
            arrived(rq.at[0:7], one.at[3])
            copy = pltpu.make_async_copy(rq, rqs, loc.at[7])
            copy.start()
            copy.wait()
            ready_asks.append(1)
        arrived(zb[c].at[0:1], zr.at[c, (hz - 1) % 2])
        for o in PARTNERS:
            e = x_slot(o)
            for zz in range(nz):
                pk[c][o, zz] = zb[c][zz, rqs[e, zz, m]]
            remote(pk[c].at[o], xr[c].at[m], one.at[1], xv.at[c], x_dev(o))
        for zz in range(nz):
            xr[c][m, zz] = zb[c][zz, rqs[m, zz, m]]

    def step_tp(b, _):
        if b == 0:
            loads[6].wait()
        for k in range(tv.shape[1]):
            tile = tv[b, k]
            high = tile.astype(BF16)
            thi[b, :, k * BS : (k + 1) * BS] = high
            tlo[b, :, k * BS : (k + 1) * BS] = (tile - high.astype(F32)).astype(BF16)

    def step_sm(c, _):
        arrived(xr[c].at[0:7], xv.at[c])
        for b in range(blocks):
            pieces = []
            for k in range(tv.shape[1]):
                col = col_ref[k, b]
                owner = col // blocks
                pieces.append(xr[c][lax.rem(owner, NX * NQ), owner // (NX * NQ)])
            value = jnp.concatenate(pieces, axis=1)
            high = value.astype(BF16).astype(F32)
            both = jnp.concatenate([high, value - high], axis=0).astype(BF16)
            first = lax.dot_general(both, thi[b], NT, preferred_element_type=F32)
            second = lax.dot_general(both, tlo[b], NT, preferred_element_type=F32)
            out_ref[c * rows : (c + 1) * rows, b * BS : (b + 1) * BS] = (
                first[0:rows] + (first[rows:] + second[0:rows]))

    steps = dict(s0=step_s0, a=step_a, fin=step_fin, zf=step_zf, xp=step_xp, tp=step_tp, sm=step_sm)
    for name, which, step in plan(chunks, hy, hz, blocks, rows):
        steps[name](which, step)
    arrived(rb[0].at[0 : 2 * hy - 1], ys.at[0])
    arrived(part.at[0 : 2 * hy - 1, :, rows:per_dest], ys.at[1])
    arrived(part.at[0 : 2 * hz - 1], one.at[0])
    arrived(part.at[0:7], one.at[1])
    arrived(rq.at[0:7], one.at[2])


def per_device(fixels, conn_tiles, columns, nuisance, nuisance_pinv, contrast, perm_table):
    ny = lax.axis_size("subj")
    nz = lax.axis_size("fix") // (NX * NQ)
    blocks, tiles = columns.shape
    fixel_count = fixels.shape[0]
    perms, regs = perm_table.shape[0], contrast.shape[0]
    cdim = perms * regs
    per_dest = cdim // ny
    chunks = per_dest // ROWS
    group = NX * NQ
    vm = pltpu.VMEM
    rc = [ROWS + (EXTRA if c == 0 else 0) for c in range(chunks)]
    hy, hz = ny // 2, nz // 2
    sem = pltpu.SemaphoreType.DMA
    scratch = [
        vm(fixels.shape, F32), vm(perm_table.shape, jnp.int32), vm(contrast.shape, F32), vm(nuisance.shape, F32),
        vm(nuisance_pinv.shape, F32), vm((nz, BS), jnp.int32), pltpu.SMEM((tiles, blocks), jnp.int32),
        vm((cdim, BS), F32), vm((cdim + 16, 3 * BS), BF16), vm((fixel_count, 3 * BS), BF16),
        vm((ny, blocks, per_dest, BS), F32), vm((blocks, EXTRA, BS), F32), vm((cdim // BS, EXTRA, BS), F32),
        vm((blocks, EXTRA, BS), F32), vm((BS, BS), F32),
        vm(conn_tiles.shape, F32), vm((blocks, BS, tiles * BS), BF16), vm((blocks, BS, tiles * BS), BF16),
        vm((group, nz, BS), jnp.int32), pltpu.SMEM((group, nz, BS), jnp.int32),
    ]
    scratch += [vm((blocks, r, BS), F32) for r in rc]
    scratch += [vm((2 * hy, blocks, r, BS), F32) for r in rc]
    scratch += [vm((nz, blocks, ROWS, BS), F32) for _ in rc]
    scratch += [vm((group, nz, ROWS, BS), F32) for _ in rc]
    scratch += [vm((group, nz, ROWS, BS), F32) for _ in rc]
    scratch += [
        sem((2,)), sem((chunks, 2)), sem((chunks, 2)), sem((chunks,)), sem((4,)), sem((8,)),
    ]
    return pl.pallas_call(
        functools.partial(kernel, ny, nz, chunks),
        out_shape=jax.ShapeDtypeStruct((per_dest, fixel_count), F32),
        in_specs=[pl.BlockSpec(memory_space=pl.ANY)] * 7,
        out_specs=pl.BlockSpec(memory_space=pltpu.VMEM),
        scratch_shapes=scratch,
        compiler_params=pltpu.CompilerParams(collective_id=0, has_side_effects=True),
        name="project_exchange",
    )(fixels, conn_tiles, perm_table, contrast, nuisance, nuisance_pinv, columns.T)


def solution(mesh):
    placed = (
        P("fix", "subj"),
        P("fix", None, None, None),
        P("fix", None),
        P(None, "subj"),
        P(None, "subj"),
        P(),
        P(None, "subj"),
    )
    return jax.shard_map(
        per_device, mesh=mesh, in_specs=placed, out_specs=P("subj", "fix"), check_vma=False
    )
```

```python
import functools

import jax
import jax.numpy as jnp
from jax import lax
from jax.experimental import pallas as pl
from jax.experimental.pallas import tpu as pltpu
from jax.sharding import PartitionSpec as P

MESH = pl.DeviceIdType.MESH
F32, BF16 = jnp.float32, jnp.bfloat16
BS = 128
NX, NQ = 4, 2
ROWS = 16
WINDOW = 4
RATE, LATENCY, GAP, SLACK = 50e3, 2.9, 0.1, 0.8
SPANS = {0: (0, 1), 1: (1, 3), 2: (3, 5), 3: (5, 7), 4: (7, 8)}
EXTRA = 8
NT = (((1,), (1,)), ((), ()))
PARTNERS = (4, 5, 2, 3, 6, 7, 1)


def plan(chunks, hy, hz, tiles, rows):
    size = rows * BS * 4 * 8
    cost = dict(s0=0.1, a=0.1, fin=0.3, zf=0.2, xp=0.1, sm=0.8, tp=0.25)
    stages = [("s0", 0)] + [("a", s) for s in range(hy - 1)] + [("fin", 0)]
    stages += [("zf", s) for s in range(hz - 1)] + [("xp", 0), ("sm", 0)]
    wire = dict(s0="y", a="y", fin="z", zf="z")
    free = dict(y=0.0, z=0.0, x=0.0)
    at, ready = [0] * chunks, [0.0] * chunks
    order, t, prepared = [], 0.0, 0

    def send(link, amount):
        free[link] = max(free[link], t) + amount / RATE + GAP
        return free[link] + LATENCY

    while any(i < len(stages) for i in at):
        best, late, soonest = None, None, 1e9
        for c in range(chunks):
            if at[c] == len(stages):
                continue
            name, when = stages[at[c]][0], ready[c]
            if name == "s0" and c and at[c - 1] == 0:
                continue
            if name == "s0" and sum(0 < i <= hy for i in at) >= WINDOW:
                continue
            if name in wire:
                when = max(when, free[wire[name]] - SLACK)
            if name == "sm":
                if prepared < tiles:
                    continue
                if when <= t and late is None:
                    late = c
            elif when <= t and best is None:
                best = c
            soonest = min(soonest, when)
        best = late if best is None else best
        if best is None:
            if prepared < tiles and order:
                order.append(("tp", prepared, 0))
                prepared += 1
                t += cost["tp"]
            else:
                t = max(soonest, t + 1e-6)
            continue
        name, step = stages[at[best]]
        order.append((name, best, step))
        t += cost[name]
        if name == "s0":
            ready[best] = send("y", size / 2)
        elif name == "a":
            ready[best] = send("y", size)
        elif name == "fin":
            ready[best] = send("z", size)
        elif name == "zf":
            ready[best] = send("z", size if step < hz - 2 else size / 2)
        span = SPANS.get({"fin": 0, "zf": step + 1, "xp": hz}.get(name))
        if span:
            last = send("x", (span[1] - span[0]) * size / 2)
            if name == "xp":
                ready[best] = last + 0.7
        at[best] += 1
    return order


def split3(value, first):
    high = value.astype(BF16)
    low = (value - high.astype(F32)).astype(BF16)
    return [high, high, low] if first else [high, low, high]


def kernel(ny, nz, chunks, *refs):
    (x_hbm, t_ref, perm_hbm, con_hbm, nui_hbm, pinv_hbm, col_hbm, out_ref), refs = refs[:8], refs[8:]
    (x_ref, perm_ref, con_ref, nui_ref, pinv_ref, req_ref, col_ref), refs = refs[:7], refs[7:]
    dsc, dcat, xcat, part, gpart, mts, gfin, mcol, tv, thi, tlo, rq, rqs = refs[:13]
    refs = refs[13:]
    sb, refs = refs[:chunks], refs[chunks:]
    rb, refs = refs[:chunks], refs[chunks:]
    zb, refs = [refs[c * nz : (c + 1) * nz] for c in range(chunks)], refs[chunks * nz :]
    pk, refs = refs[:chunks], refs[chunks:]
    xr, refs = refs[:chunks], refs[chunks:]
    ys, yr, zr, xv, one, loc = refs
    hy, hz = ny // 2, nz // 2
    blocks = x_ref.shape[0] // BS
    half = blocks // 2
    rows = ROWS
    per_dest = rows * chunks
    perms = perm_ref.shape[0]
    regs = con_ref.shape[0]
    nuis = nui_ref.shape[0]
    cdim = perms * regs

    fix, y = lax.axis_index("fix"), lax.axis_index("subj")
    q = lax.rem(fix, NQ)
    x = lax.rem(fix // NQ, NX)
    z = fix // (NQ * NX)
    m = x * NQ + q

    def fix_of(zz, xx, qq):
        return (zz * NX + xx) * NQ + qq

    x_by = {0: x, 1: x + 1 - 2 * lax.rem(x, 2), 2: lax.rem(x + 2, NX), 3: NX - 1 - x}
    q_by = {0: q, 1: 1 - q}
    y_to = [lax.rem(y + 1, ny), lax.rem(y + ny - 1, ny)]
    z_to = [lax.rem(z + 1, nz), lax.rem(z + nz - 1, nz)]

    def y_dev(d):
        return (fix, y_to[d])

    def z_dev(d):
        return (fix_of(z_to[d], x, q), y)

    def x_dev(o):
        return (fix_of(z, x_by[o // 2], q_by[o % 2]), y)

    def x_slot(o):
        return x_by[o // 2] * NQ + q_by[o % 2]

    peers = [y_dev(0), y_dev(1), z_dev(0), z_dev(1)] + [x_dev(o) for o in range(1, 8)]
    barrier = pltpu.get_barrier_semaphore()
    for peer in peers:
        pl.semaphore_signal(barrier, inc=1, device_id=peer, device_id_type=MESH)

    loads = []
    for i, (src, dst) in enumerate((
        (perm_hbm, perm_ref), (con_hbm, con_ref), (x_hbm, x_ref), (nui_hbm, nui_ref),
        (pinv_hbm, pinv_ref), (col_hbm, col_ref), (t_ref, tv),
    )):
        loads.append(pltpu.make_async_copy(src, dst, loc.at[i]))
        loads[-1].start()

    def arrived(ref, sem):
        pltpu.make_async_copy(ref, ref, sem).wait()

    def remote(src, dst, send_sem, recv_sem, device):
        copy = pltpu.make_async_remote_copy(
            src_ref=src, dst_ref=dst, send_sem=send_sem, recv_sem=recv_sem,
            device_id=device, device_id_type=MESH,
        )
        copy.start()

    loads[0].wait()
    loads[1].wait()
    index = perm_ref[...]
    group, lane = index // BS, lax.rem(index, BS)
    for r in range(regs):
        picked = jnp.zeros((perms, BS), F32)
        for g in range(con_ref.shape[1] // BS):
            table = jnp.broadcast_to(con_ref[r : r + 1, g * BS : (g + 1) * BS], (perms, BS))
            value = jnp.take_along_axis(table, lane, axis=1, mode="promise_in_bounds")
            picked = jnp.where(group == g, value, picked)
        dsc[pl.ds(r, perms, stride=regs), :] = picked
    for i, piece in enumerate(split3(dsc[...], True)):
        dcat[0:cdim, i * BS : (i + 1) * BS] = piece
    for i in range(2, 6):
        loads[i].wait()
    pinv = jnp.concatenate([pinv_ref[...], jnp.zeros((16 - nuis, BS), F32)], axis=0)
    for i, piece in enumerate(split3(pinv, True)):
        dcat[cdim : cdim + 16, i * BS : (i + 1) * BS] = piece
    for i, piece in enumerate(split3(x_ref[...], False)):
        xcat[:, i * BS : (i + 1) * BS] = piece
    nui = jnp.concatenate([jnp.zeros((nuis, BS), F32), nui_ref[...], jnp.zeros((16 - 2 * nuis, BS), F32)], axis=0)
    ncat = jnp.concatenate(split3(nui, False), axis=1)
    load = lax.dot_general(ncat, dcat[0:cdim, :], NT, preferred_element_type=F32)
    for i in range(cdim // BS):
        mts[i] = load[0:EXTRA, i * BS : (i + 1) * BS]
    for b in range(0, blocks, 2):
        both = lax.dot_general(dcat[...], xcat[b * BS : (b + 2) * BS, :], NT, preferred_element_type=F32)
        for i in range(2):
            mine = both[:, i * BS : (i + 1) * BS]
            part[:, b + i] = mine[0:cdim].reshape(ny, per_dest, BS)
            gpart[b + i] = mine[cdim : cdim + EXTRA]

    def store_own(ref, dest, c, lo, hi, add):
        top = part[dest, lo:hi, c * rows : (c + 1) * rows, :]
        ref[lo:hi, 0:rows, :] = ref[lo:hi, 0:rows, :] + top if add else top
        if c == 0:
            more = gpart[lo:hi]
            ref[lo:hi, rows : rows + EXTRA, :] = ref[lo:hi, rows : rows + EXTRA, :] + more if add else more
            if lo == 0:
                per = BS // per_dest
                ref[0, rows : rows + EXTRA, :] = ref[0, rows : rows + EXTRA, :] + mts[dest // per]

    line = lax.broadcasted_iota(jnp.int32, (nz, BS), 0)
    place = lax.broadcasted_iota(jnp.int32, (nz, BS), 1)
    place = jnp.where(place < NX * NQ, line * (NX * NQ) + place, -1)
    request = jnp.zeros((nz, BS), jnp.int32)
    for b in range(blocks):
        for k in range(tv.shape[1]):
            col = col_ref[k, b]
            request = jnp.where(place == col // blocks, lax.rem(col, blocks), request)
    req_ref[...] = request
    rq[m] = request

    pl.semaphore_wait(barrier, len(peers))

    def step_s0(c, _):
        store_own(sb[c], lax.rem(y + hy, ny), c, 0, blocks, False)
        out = ys.at[min(c, 1)]
        remote(sb[c].at[0:half], rb[c].at[0, 0:half], out, yr.at[c, 0], y_dev(0))
        remote(sb[c].at[half:blocks], rb[c].at[1, half:blocks], out, yr.at[c, 0], y_dev(1))
        if c == 0:
            for o in range(1, 8):
                remote(req_ref, rq.at[m], one.at[2], one.at[3], x_dev(o))

    def step_a(c, s):
        arrived(rb[c].at[0] if s == 0 else rb[c].at[0:2], yr.at[c, s % 2])
        for d in range(2):
            far = hy - 1 - s
            dest = lax.rem(y + (far if d == 0 else ny - far), ny)
            held = rb[c].at[2 * s + d]
            if s == 0:
                lo, hi = (0, half) if d == 0 else (half, blocks)
                store_own(held, dest, c, lo, hi, True)
                other = (half, blocks) if d == 0 else (0, half)
                store_own(held, dest, c, other[0], other[1], False)
            else:
                store_own(held, dest, c, 0, blocks, True)
            remote(held, rb[c].at[2 * s + 2 + d], ys.at[min(c, 1)], yr.at[c, (s + 1) % 2], y_dev(d))

    def z_send(c, s, d):
        mine, theirs = ((nz - s) % nz, (nz - s - 1) % nz) if d == 0 else (s, s + 1)
        src, dst = zb[c][mine], zb[c][theirs]
        if s == hz - 1:
            lo, hi = (0, half) if d == 0 else (half, blocks)
            src, dst = src.at[lo:hi], dst.at[lo:hi]
        remote(src, dst, one.at[0], zr.at[c, s % 2], z_dev(d))

    slots = [0]
    for far in range(1, hz):
        slots += [far, nz - far]
    slots.append(hz)
    z_of = [lax.rem(z + slots[i], nz) for i in range(nz)]
    ready_asks = []

    def x_send(c, stage):
        if not ready_asks:
            arrived(rq.at[0:7], one.at[3])
            copy = pltpu.make_async_copy(rq, rqs, loc.at[7])
            copy.start()
            copy.wait()
            ready_asks.append(1)
        if stage not in SPANS:
            return
        lo, hi = SPANS[stage]
        for o in PARTNERS:
            e = x_slot(o)
            for i in range(lo, hi):
                pk[c][o, i] = zb[c][slots[i]][rqs[e, z_of[i], m]]
            remote(pk[c].at[o, lo:hi], xr[c].at[m, lo:hi], one.at[1], xv.at[c], x_dev(o))
        for i in range(lo, hi):
            xr[c][m, i] = zb[c][slots[i]][rqs[m, z_of[i], m]]

    def step_fin(c, _):
        arrived(rb[c].at[0:2], yr.at[c, (hy - 1) % 2])
        held = rb[c].at[2 * hy - 2]
        store_own(held, y, c, 0, blocks, True)
        if c == 0:
            more = held[:, rows : rows + EXTRA, :] + rb[c][2 * hy - 1, :, rows : rows + EXTRA, :]
            gfin[...] = more
            square = jnp.concatenate([more[0], jnp.zeros((BS - EXTRA, BS), F32)], axis=0)
            mcol[...] = jnp.transpose(square)
        total = held[:, 0:rows, :] + rb[c][2 * hy - 1, :, 0:rows, :]
        per = BS // per_dest
        cols = mcol[pl.ds(lax.rem(y, per) * per_dest + c * rows, rows), :]
        for n in range(nuis):
            weight = jnp.broadcast_to(cols[:, nuis + n : nuis + n + 1], (rows, BS))
            total = total - weight[None] * gfin[:, n : n + 1, :]
        zb[c][0][...] = total
        for d in range(2):
            z_send(c, 0, d)
        x_send(c, 0)

    def step_zf(c, s):
        arrived(part.at[0:2, :, 0:rows], zr.at[c, s % 2])
        for d in range(2):
            z_send(c, s + 1, d)
        x_send(c, s + 1)

    def step_xp(c, _):
        arrived(part.at[0:1, :, 0:rows], zr.at[c, (hz - 1) % 2])
        x_send(c, hz)

    def step_tp(b, _):
        if b == 0:
            loads[6].wait()
        for k in range(tv.shape[1]):
            tile = tv[b, k]
            high = tile.astype(BF16)
            thi[b, :, k * BS : (k + 1) * BS] = high
            tlo[b, :, k * BS : (k + 1) * BS] = (tile - high.astype(F32)).astype(BF16)

    found = []

    def find():
        for b in range(blocks):
            for k in range(tv.shape[1]):
                owner = col_ref[k, b] // blocks
                far = lax.rem(owner // (NX * NQ) + nz - z, nz)
                slot = jnp.where(far < hz, jnp.maximum(2 * far - 1, 0), jnp.where(far == hz, nz - 1, 2 * (nz - far)))
                found.append((lax.rem(owner, NX * NQ), slot))

    def step_sm(c, _):
        if not found:
            find()
        arrived(xr[c].at[0:7], xv.at[c])
        for b in range(blocks):
            pieces = []
            for k in range(tv.shape[1]):
                who, slot = found[b * tv.shape[1] + k]
                pieces.append(xr[c][who, slot])
            value = jnp.concatenate(pieces, axis=1)
            high = value.astype(BF16).astype(F32)
            both = jnp.concatenate([high, value - high], axis=0).astype(BF16)
            first = lax.dot_general(both, thi[b], NT, preferred_element_type=F32)
            second = lax.dot_general(both, tlo[b], NT, preferred_element_type=F32)
            out_ref[c * rows : (c + 1) * rows, b * BS : (b + 1) * BS] = (
                first[0:rows] + (first[rows:] + second[0:rows]))

    steps = dict(s0=step_s0, a=step_a, fin=step_fin, zf=step_zf, xp=step_xp, tp=step_tp, sm=step_sm)
    for name, which, step in plan(chunks, hy, hz, blocks, rows):
        steps[name](which, step)
    arrived(rb[0].at[0 : 2 * hy - 1], ys.at[0])
    arrived(part.at[0 : 2 * hy - 1, :, rows:per_dest], ys.at[1])
    arrived(part.at[0 : 2 * hz - 1], one.at[0])
    arrived(part.at[0:7], one.at[1])
    arrived(rq.at[0:7], one.at[2])


def per_device(fixels, conn_tiles, columns, nuisance, nuisance_pinv, contrast, perm_table):
    ny = lax.axis_size("subj")
    nz = lax.axis_size("fix") // (NX * NQ)
    blocks, tiles = columns.shape
    fixel_count = fixels.shape[0]
    perms, regs = perm_table.shape[0], contrast.shape[0]
    cdim = perms * regs
    per_dest = cdim // ny
    chunks = per_dest // ROWS
    group = NX * NQ
    vm = pltpu.VMEM
    rc = [ROWS + (EXTRA if c == 0 else 0) for c in range(chunks)]
    hy, hz = ny // 2, nz // 2
    sem = pltpu.SemaphoreType.DMA
    scratch = [
        vm(fixels.shape, F32), vm(perm_table.shape, jnp.int32), vm(contrast.shape, F32), vm(nuisance.shape, F32),
        vm(nuisance_pinv.shape, F32), vm((nz, BS), jnp.int32), pltpu.SMEM((tiles, blocks), jnp.int32),
        vm((cdim, BS), F32), vm((cdim + 16, 3 * BS), BF16), vm((fixel_count, 3 * BS), BF16),
        vm((ny, blocks, per_dest, BS), F32), vm((blocks, EXTRA, BS), F32), vm((cdim // BS, EXTRA, BS), F32),
        vm((blocks, EXTRA, BS), F32), vm((BS, BS), F32),
        vm(conn_tiles.shape, F32), vm((blocks, BS, tiles * BS), BF16), vm((blocks, BS, tiles * BS), BF16),
        vm((group, nz, BS), jnp.int32), pltpu.SMEM((group, nz, BS), jnp.int32),
    ]
    scratch += [vm((blocks, r, BS), F32) for r in rc]
    scratch += [vm((2 * hy, blocks, r, BS), F32) for r in rc]
    scratch += [vm((blocks, ROWS, BS), F32) for _ in rc for _ in range(nz)]
    scratch += [vm((group, nz, ROWS, BS), F32) for _ in rc]
    scratch += [vm((group, nz, ROWS, BS), F32) for _ in rc]
    scratch += [
        sem((2,)), sem((chunks, 2)), sem((chunks, 2)), sem((chunks,)), sem((4,)), sem((8,)),
    ]
    return pl.pallas_call(
        functools.partial(kernel, ny, nz, chunks),
        out_shape=jax.ShapeDtypeStruct((per_dest, fixel_count), F32),
        in_specs=[pl.BlockSpec(memory_space=pl.ANY)] * 7,
        out_specs=pl.BlockSpec(memory_space=pltpu.VMEM),
        scratch_shapes=scratch,
        compiler_params=pltpu.CompilerParams(collective_id=0, has_side_effects=True),
        name="project_exchange",
    )(fixels, conn_tiles, perm_table, contrast, nuisance, nuisance_pinv, columns.T)


def solution(mesh):
    placed = (
        P("fix", "subj"),
        P("fix", None, None, None),
        P("fix", None),
        P(None, "subj"),
        P(None, "subj"),
        P(),
        P(None, "subj"),
    )
    return jax.shard_map(
        per_device, mesh=mesh, in_specs=placed, out_specs=P("subj", "fix"), check_vma=False
    )
```

```python
import functools

import jax
import jax.numpy as jnp
from jax import lax
from jax.experimental import pallas as pl
from jax.experimental.pallas import tpu as pltpu
from jax.sharding import PartitionSpec as P

MESH = pl.DeviceIdType.MESH
F32, BF16 = jnp.float32, jnp.bfloat16
BS = 128
NX, NQ = 4, 2
ROWS = 16
WINDOW = 4
RATE, LATENCY, GAP, SLACK = 50e3, 2.9, 0.1, 0.8
SPANS = {0: (0, 1), 1: (1, 3), 2: (3, 5), 3: (5, 7), 4: (7, 8)}
EXTRA = 8
NT = (((1,), (1,)), ((), ()))
PARTNERS = (4, 5, 2, 3, 6, 7, 1)


def plan(chunks, hy, hz, tiles, rows):
    size = rows * BS * 4 * 8
    cost = dict(s0=0.1, a=0.1, fin=0.3, zf=0.2, xp=0.1, sm=0.8, tp=0.25)
    stages = [("s0", 0)] + [("a", s) for s in range(hy - 1)] + [("fin", 0)]
    stages += [("zf", s) for s in range(hz - 1)] + [("xp", 0), ("sm", 0)]
    wire = dict(s0="y", a="y", fin="z", zf="z")
    free = dict(y=0.0, z=0.0, x=0.0)
    at, ready = [0] * chunks, [0.0] * chunks
    order, t, prepared = [], 0.0, 0

    def send(link, amount):
        free[link] = max(free[link], t) + amount / RATE + GAP
        return free[link] + LATENCY

    while any(i < len(stages) for i in at):
        best, late, soonest = None, None, 1e9
        for c in range(chunks):
            if at[c] == len(stages):
                continue
            name, when = stages[at[c]][0], ready[c]
            if name == "s0" and c and at[c - 1] == 0:
                continue
            if name == "s0" and sum(0 < i <= hy for i in at) >= WINDOW:
                continue
            if name in wire:
                when = max(when, free[wire[name]] - SLACK)
            if name == "sm":
                if prepared < tiles:
                    continue
                if when <= t and late is None:
                    late = c
            elif when <= t and best is None:
                best = c
            soonest = min(soonest, when)
        best = late if best is None else best
        if best is None:
            if prepared < tiles and order:
                order.append(("tp", prepared, 0))
                prepared += 1
                t += cost["tp"]
            else:
                t = max(soonest, t + 1e-6)
            continue
        name, step = stages[at[best]]
        order.append((name, best, step))
        t += cost[name]
        if name == "s0":
            ready[best] = send("y", size / 2)
        elif name == "a":
            ready[best] = send("y", size)
        elif name == "fin":
            ready[best] = send("z", size)
        elif name == "zf":
            ready[best] = send("z", size if step < hz - 2 else size / 2)
        span = SPANS.get({"fin": 0, "zf": step + 1, "xp": hz}.get(name))
        if span:
            last = send("x", (span[1] - span[0]) * size / 2)
            if name == "xp":
                ready[best] = last + 0.7
        at[best] += 1
    return order


def split3(value, first):
    high = value.astype(BF16)
    low = (value - high.astype(F32)).astype(BF16)
    return [high, high, low] if first else [high, low, high]


def kernel(ny, nz, chunks, *refs):
    (x_hbm, t_ref, perm_hbm, con_hbm, nui_hbm, pinv_hbm, col_hbm, out_ref), refs = refs[:8], refs[8:]
    (x_ref, perm_ref, con_ref, nui_ref, pinv_ref, req_ref, col_ref), refs = refs[:7], refs[7:]
    dsc, dcat, xcat, part, gpart, mts, gfin, mcol, tv, tcat, rq, rqs, eb, es = refs[:14]
    refs = refs[14:]
    sb, refs = refs[:chunks], refs[chunks:]
    rb, refs = refs[:chunks], refs[chunks:]
    zb, refs = [refs[c * nz : (c + 1) * nz] for c in range(chunks)], refs[chunks * nz :]
    pk, refs = refs[:chunks], refs[chunks:]
    xr, refs = refs[:chunks], refs[chunks:]
    er, yr, zr, xv, one, loc = refs
    hy, hz = ny // 2, nz // 2
    blocks = x_ref.shape[0] // BS
    half = blocks // 2
    rows = ROWS
    per_dest = rows * chunks
    perms = perm_ref.shape[0]
    regs = con_ref.shape[0]
    nuis = nui_ref.shape[0]
    cdim = perms * regs

    fix, y = lax.axis_index("fix"), lax.axis_index("subj")
    q = lax.rem(fix, NQ)
    x = lax.rem(fix // NQ, NX)
    z = fix // (NQ * NX)
    m = x * NQ + q

    def fix_of(zz, xx, qq):
        return (zz * NX + xx) * NQ + qq

    x_by = {0: x, 1: x + 1 - 2 * lax.rem(x, 2), 2: lax.rem(x + 2, NX), 3: NX - 1 - x}
    q_by = {0: q, 1: 1 - q}
    y_to = [lax.rem(y + 1, ny), lax.rem(y + ny - 1, ny)]
    z_to = [lax.rem(z + 1, nz), lax.rem(z + nz - 1, nz)]

    def y_dev(d):
        return (fix, y_to[d])

    def z_dev(d):
        return (fix_of(z_to[d], x, q), y)

    def x_dev(o):
        return (fix_of(z, x_by[o // 2], q_by[o % 2]), y)

    def x_slot(o):
        return x_by[o // 2] * NQ + q_by[o % 2]

    peers = [y_dev(0), y_dev(1), z_dev(0), z_dev(1)] + [x_dev(o) for o in range(1, 8)]
    barrier = pltpu.get_barrier_semaphore()
    for peer in peers:
        pl.semaphore_signal(barrier, inc=1, device_id=peer, device_id_type=MESH)

    loads = []
    for i, (src, dst) in enumerate((
        (perm_hbm, perm_ref), (con_hbm, con_ref), (x_hbm, x_ref), (nui_hbm, nui_ref),
        (pinv_hbm, pinv_ref), (col_hbm, col_ref), (t_ref, tv),
    )):
        loads.append(pltpu.make_async_copy(src, dst, loc.at[i]))
        loads[-1].start()

    def arrived(ref, sem):
        pltpu.make_async_copy(ref, ref, sem).wait()

    def remote(src, dst, send_sem, recv_sem, device):
        copy = pltpu.make_async_remote_copy(
            src_ref=src, dst_ref=dst, send_sem=send_sem, recv_sem=recv_sem,
            device_id=device, device_id_type=MESH,
        )
        copy.start()

    loads[0].wait()
    loads[1].wait()
    index = perm_ref[...]
    group, lane = index // BS, lax.rem(index, BS)
    for r in range(regs):
        picked = jnp.zeros((perms, BS), F32)
        for g in range(con_ref.shape[1] // BS):
            table = jnp.broadcast_to(con_ref[r : r + 1, g * BS : (g + 1) * BS], (perms, BS))
            value = jnp.take_along_axis(table, lane, axis=1, mode="promise_in_bounds")
            picked = jnp.where(group == g, value, picked)
        dsc[pl.ds(r, perms, stride=regs), :] = picked
    for i, piece in enumerate(split3(dsc[...], True)):
        dcat[0:cdim, i * BS : (i + 1) * BS] = piece
    for i in range(2, 6):
        loads[i].wait()
    gap = jnp.zeros((EXTRA - nuis, BS), F32)
    pinv = jnp.concatenate([pinv_ref[...], gap, gap, pinv_ref[...]], axis=0)
    for i, piece in enumerate(split3(pinv, True)):
        dcat[cdim : cdim + 16, i * BS : (i + 1) * BS] = piece
    for i, piece in enumerate(split3(x_ref[...], False)):
        xcat[:, i * BS : (i + 1) * BS] = piece
    nui = jnp.concatenate([jnp.zeros((nuis, BS), F32), nui_ref[...], jnp.zeros((16 - 2 * nuis, BS), F32)], axis=0)
    ncat = jnp.concatenate(split3(nui, False), axis=1)
    load = lax.dot_general(ncat, dcat[0:cdim, :], NT, preferred_element_type=F32)
    for i in range(cdim // BS):
        mts[i] = load[0:EXTRA, i * BS : (i + 1) * BS]
    far_dest = lax.rem(y + hy, ny)
    first = jnp.concatenate(
        [dcat[pl.ds(pl.multiple_of(far_dest * per_dest, per_dest), per_dest), :], dcat[cdim : cdim + 16, :]], axis=0)
    for b in range(0, blocks, 2):
        both = lax.dot_general(first, xcat[b * BS : (b + 2) * BS, :], NT, preferred_element_type=F32)
        for c in range(chunks):
            for i in range(2):
                sb[c][b + i] = both[c * rows : (c + 1) * rows, i * BS : (i + 1) * BS]
        gpart[b // 2] = both[per_dest : per_dest + EXTRA, 0:BS] + both[per_dest + EXTRA :, BS : 2 * BS]

    def store_own(ref, dest, c, lo, hi, add):
        top = part[dest, lo:hi, c * rows : (c + 1) * rows, :]
        ref[lo:hi, 0:rows, :] = ref[lo:hi, 0:rows, :] + top if add else top

    et = gpart.shape[0] + 1
    eh = et // 2
    per = BS // per_dest

    def store_extra(ref, dest, lo, hi, add):
        for i in range(lo, hi):
            value = gpart[i] if i < et - 1 else mts[dest // per]
            ref[i] = ref[i] + value if add else value

    line = lax.broadcasted_iota(jnp.int32, (nz, BS), 0)
    place = lax.broadcasted_iota(jnp.int32, (nz, BS), 1)
    place = jnp.where(place < NX * NQ, line * (NX * NQ) + place, -1)
    request = jnp.zeros((nz, BS), jnp.int32)
    for b in range(blocks):
        for k in range(tv.shape[1]):
            col = col_ref[k, b]
            request = jnp.where(place == col // blocks, lax.rem(col, blocks), request)
    req_ref[...] = request
    rq[m] = request

    pl.semaphore_wait(barrier, len(peers))

    def step_s0(c, _):
        out = one.at[4]
        if c == 0:
            store_extra(es, far_dest, 0, et, False)
            remote(es.at[0:eh], eb.at[0, 0:eh], one.at[5], er.at[0], y_dev(0))
            remote(es.at[eh:et], eb.at[1, eh:et], one.at[5], er.at[0], y_dev(1))
        remote(sb[c].at[0:half], rb[c].at[0, 0:half], out, yr.at[c, 0], y_dev(0))
        remote(sb[c].at[half:blocks], rb[c].at[1, half:blocks], out, yr.at[c, 0], y_dev(1))
        if c == 0:
            for o in range(1, 8):
                remote(req_ref, rq.at[m], one.at[2], one.at[3], x_dev(o))

    def dest_of(s, d):
        far = hy - 1 - s
        return lax.rem(y + (far if d == 0 else ny - far), ny)

    def step_a(c, s):
        if c == 0:
            arrived(eb.at[0] if s == 0 else eb.at[0:2], er.at[s % 2])
            for d in range(2):
                held = eb.at[2 * s + d]
                lo, hi = (0, et) if s else ((0, eh) if d == 0 else (eh, et))
                store_extra(held, dest_of(s, d), lo, hi, True)
                if s == 0:
                    store_extra(held, dest_of(s, d), hi % et, lo if lo else et, False)
                remote(held, eb.at[2 * s + 2 + d], one.at[5], er.at[(s + 1) % 2], y_dev(d))
        arrived(rb[c].at[0] if s == 0 else rb[c].at[0:2], yr.at[c, s % 2])
        for d in range(2):
            dest = dest_of(s, d)
            held = rb[c].at[2 * s + d]
            if s == 0:
                lo, hi = (0, half) if d == 0 else (half, blocks)
                store_own(held, dest, c, lo, hi, True)
                other = (half, blocks) if d == 0 else (0, half)
                store_own(held, dest, c, other[0], other[1], False)
            else:
                store_own(held, dest, c, 0, blocks, True)
            remote(held, rb[c].at[2 * s + 2 + d], one.at[4], yr.at[c, (s + 1) % 2], y_dev(d))

    def z_send(c, s, d):
        mine, theirs = ((nz - s) % nz, (nz - s - 1) % nz) if d == 0 else (s, s + 1)
        src, dst = zb[c][mine], zb[c][theirs]
        if s == hz - 1:
            lo, hi = (0, half) if d == 0 else (half, blocks)
            src, dst = src.at[lo:hi], dst.at[lo:hi]
        remote(src, dst, one.at[0], zr.at[c, s % 2], z_dev(d))

    slots = [0]
    for far in range(1, hz):
        slots += [far, nz - far]
    slots.append(hz)
    z_of = [lax.rem(z + slots[i], nz) for i in range(nz)]
    ready_asks = []

    def x_send(c, stage):
        if not ready_asks:
            arrived(rq.at[0:7], one.at[3])
            copy = pltpu.make_async_copy(rq, rqs, loc.at[7])
            copy.start()
            copy.wait()
            ready_asks.append(1)
        if stage not in SPANS:
            return
        lo, hi = SPANS[stage]
        for o in PARTNERS:
            e = x_slot(o)
            for i in range(lo, hi):
                pk[c][o, i] = zb[c][slots[i]][rqs[e, z_of[i], m]]
            remote(pk[c].at[o, lo:hi], xr[c].at[m, lo:hi], one.at[1], xv.at[c], x_dev(o))
        for i in range(lo, hi):
            xr[c][m, i] = zb[c][slots[i]][rqs[m, z_of[i], m]]

    def step_fin(c, _):
        arrived(rb[c].at[0:2], yr.at[c, (hy - 1) % 2])
        held = rb[c].at[2 * hy - 2]
        store_own(held, y, c, 0, blocks, True)
        if c == 0:
            arrived(eb.at[0:2], er.at[(hy - 1) % 2])
            last = eb.at[2 * hy - 2]
            store_extra(last, y, 0, et, True)
            for i in range(et - 1):
                more = last[i] + eb[2 * hy - 1, i]
                gfin[2 * i, 0:nuis, :] = more[0:nuis]
                gfin[2 * i + 1, 0:nuis, :] = more[nuis : 2 * nuis]
            square = jnp.concatenate(
                [last[et - 1] + eb[2 * hy - 1, et - 1], jnp.zeros((BS - EXTRA, BS), F32)], axis=0)
            mcol[...] = jnp.transpose(square)
        total = held[:, 0:rows, :] + rb[c][2 * hy - 1, :, 0:rows, :]
        cols = mcol[pl.ds(lax.rem(y, per) * per_dest + c * rows, rows), :]
        for n in range(nuis):
            weight = jnp.broadcast_to(cols[:, nuis + n : nuis + n + 1], (rows, BS))
            total = total - weight[None] * gfin[:, n : n + 1, :]
        zb[c][0][...] = total
        for d in range(2):
            z_send(c, 0, d)
        x_send(c, 0)

    def step_zf(c, s):
        arrived(part.at[0:2, :, 0:rows], zr.at[c, s % 2])
        for d in range(2):
            z_send(c, s + 1, d)
        x_send(c, s + 1)

    def step_xp(c, _):
        arrived(part.at[0:1, :, 0:rows], zr.at[c, (hz - 1) % 2])
        x_send(c, hz)

    def step_tp(b, _):
        if b == 0:
            loads[6].wait()
        for k in range(tv.shape[1]):
            tile = tv[b, k]
            high = tile.astype(BF16)
            tcat[b, 0:BS, k * BS : (k + 1) * BS] = high
            tcat[b, BS : 2 * BS, k * BS : (k + 1) * BS] = (tile - high.astype(F32)).astype(BF16)

    found = []

    def find():
        for b in range(blocks):
            for k in range(tv.shape[1]):
                owner = col_ref[k, b] // blocks
                far = lax.rem(owner // (NX * NQ) + nz - z, nz)
                slot = jnp.where(far < hz, jnp.maximum(2 * far - 1, 0), jnp.where(far == hz, nz - 1, 2 * (nz - far)))
                found.append((lax.rem(owner, NX * NQ), slot))

    def step_sm(c, _):
        if not found:
            find()
        arrived(xr[c].at[0:7], xv.at[c])
        for b in range(blocks):
            pieces = []
            for k in range(tv.shape[1]):
                who, slot = found[b * tv.shape[1] + k]
                pieces.append(xr[c][who, slot])
            value = jnp.concatenate(pieces, axis=1)
            high = value.astype(BF16).astype(F32)
            both = jnp.concatenate([high, value - high], axis=0).astype(BF16)
            got = lax.dot_general(both, tcat[b], NT, preferred_element_type=F32)
            out_ref[c * rows : (c + 1) * rows, b * BS : (b + 1) * BS] = got[0:rows, 0:BS] + (
                got[rows:, 0:BS] + got[0:rows, BS:] + got[rows:, BS:])

    steps = dict(s0=step_s0, a=step_a, fin=step_fin, zf=step_zf, xp=step_xp, tp=step_tp, sm=step_sm)
    for c in range(chunks):
        step_s0(c, 0)
    for b in range(0, blocks, 2):
        both = lax.dot_general(dcat[0:cdim, :], xcat[b * BS : (b + 2) * BS, :], NT, preferred_element_type=F32)
        for i in range(2):
            part[:, b + i] = both[:, i * BS : (i + 1) * BS].reshape(ny, per_dest, BS)
    for name, which, step in plan(chunks, hy, hz, blocks, rows):
        if name != "s0":
            steps[name](which, step)
    arrived(part.at[0 : 2 * hy - 1], one.at[4])
    arrived(eb.at[0 : 2 * hy - 1], one.at[5])
    arrived(part.at[0 : 2 * hz - 1], one.at[0])
    arrived(part.at[0:7], one.at[1])
    arrived(rq.at[0:7], one.at[2])


def per_device(fixels, conn_tiles, columns, nuisance, nuisance_pinv, contrast, perm_table):
    ny = lax.axis_size("subj")
    nz = lax.axis_size("fix") // (NX * NQ)
    blocks, tiles = columns.shape
    fixel_count = fixels.shape[0]
    perms, regs = perm_table.shape[0], contrast.shape[0]
    cdim = perms * regs
    per_dest = cdim // ny
    chunks = per_dest // ROWS
    group = NX * NQ
    vm = pltpu.VMEM
    rc = [ROWS] * chunks
    hy = ny // 2
    extra = blocks // 2 + 1
    sem = pltpu.SemaphoreType.DMA
    scratch = [
        vm(fixels.shape, F32), vm(perm_table.shape, jnp.int32), vm(contrast.shape, F32), vm(nuisance.shape, F32),
        vm(nuisance_pinv.shape, F32), vm((nz, BS), jnp.int32), pltpu.SMEM((tiles, blocks), jnp.int32),
        vm((cdim, BS), F32), vm((cdim + 16, 3 * BS), BF16), vm((fixel_count, 3 * BS), BF16),
        vm((ny, blocks, per_dest, BS), F32), vm((blocks // 2, EXTRA, BS), F32), vm((cdim // BS, EXTRA, BS), F32),
        vm((blocks, EXTRA, BS), F32), vm((BS, BS), F32),
        vm(conn_tiles.shape, F32), vm((blocks, 2 * BS, tiles * BS), BF16),
        vm((group, nz, BS), jnp.int32), pltpu.SMEM((group, nz, BS), jnp.int32),
        vm((2 * hy, extra, EXTRA, BS), F32), vm((extra, EXTRA, BS), F32),
    ]
    scratch += [vm((blocks, r, BS), F32) for r in rc]
    scratch += [vm((2 * hy, blocks, r, BS), F32) for r in rc]
    scratch += [vm((blocks, ROWS, BS), F32) for _ in rc for _ in range(nz)]
    scratch += [vm((group, nz, ROWS, BS), F32) for _ in rc]
    scratch += [vm((group, nz, ROWS, BS), F32) for _ in rc]
    scratch += [
        sem((2,)), sem((chunks, 2)), sem((chunks, 2)), sem((chunks,)), sem((6,)), sem((8,)),
    ]
    return pl.pallas_call(
        functools.partial(kernel, ny, nz, chunks),
        out_shape=jax.ShapeDtypeStruct((per_dest, fixel_count), F32),
        in_specs=[pl.BlockSpec(memory_space=pl.ANY)] * 7,
        out_specs=pl.BlockSpec(memory_space=pltpu.VMEM),
        scratch_shapes=scratch,
        compiler_params=pltpu.CompilerParams(collective_id=0, has_side_effects=True),
        name="project_exchange",
    )(fixels, conn_tiles, perm_table, contrast, nuisance, nuisance_pinv, columns.T)


def solution(mesh):
    placed = (
        P("fix", "subj"),
        P("fix", None, None, None),
        P("fix", None),
        P(None, "subj"),
        P(None, "subj"),
        P(),
        P(None, "subj"),
    )
    return jax.shard_map(
        per_device, mesh=mesh, in_specs=placed, out_specs=P("subj", "fix"), check_vma=False
    )
```

```python
import functools

import jax
import jax.numpy as jnp
from jax import lax
from jax.experimental import pallas as pl
from jax.experimental.pallas import tpu as pltpu
from jax.sharding import PartitionSpec as P

MESH = pl.DeviceIdType.MESH
F32, BF16 = jnp.float32, jnp.bfloat16
BS = 128
NX, NQ = 4, 2
ROWS = 16
WINDOW = 4
RATE, LATENCY, GAP, SLACK = 50e3, 2.9, 0.1, 0.8
SPANS = {0: (0, 1), 1: (1, 3), 2: (3, 5), 3: (5, 7), 4: (7, 8)}
EXTRA = 8
NT = (((1,), (1,)), ((), ()))
PARTNERS = (4, 5, 2, 3, 6, 7, 1)


def plan(chunks, hy, hz, tiles, rows):
    size = rows * BS * 4 * 8
    cost = dict(s0=0.1, a=0.1, fin=0.3, zf=0.2, xp=0.1, sm=0.8, tp=0.25)
    stages = [("s0", 0)] + [("a", s) for s in range(hy - 1)] + [("fin", 0)]
    stages += [("zf", s) for s in range(hz - 1)] + [("xp", 0), ("sm", 0)]
    wire = dict(s0="y", a="y", fin="z", zf="z")
    free = dict(y=0.0, z=0.0, x=0.0)
    at, ready = [0] * chunks, [0.0] * chunks
    order, t, prepared = [], 0.0, 0

    def send(link, amount):
        free[link] = max(free[link], t) + amount / RATE + GAP
        return free[link] + LATENCY

    while any(i < len(stages) for i in at):
        best, late, soonest = None, None, 1e9
        for c in range(chunks):
            if at[c] == len(stages):
                continue
            name, when = stages[at[c]][0], ready[c]
            if name == "s0" and c and at[c - 1] == 0:
                continue
            if name == "s0" and sum(0 < i <= hy for i in at) >= WINDOW:
                continue
            if name in wire:
                when = max(when, free[wire[name]] - SLACK)
            if name == "sm":
                if prepared < tiles:
                    continue
                if when <= t and late is None:
                    late = c
            elif when <= t and best is None:
                best = c
            soonest = min(soonest, when)
        best = late if best is None else best
        if best is None:
            if prepared < tiles and len(order) > 2 * chunks:
                order.append(("tp", prepared, 0))
                prepared += 1
                t += cost["tp"]
            else:
                t = max(soonest, t + 1e-6)
            continue
        name, step = stages[at[best]]
        order.append((name, best, step))
        t += cost[name]
        if name == "s0":
            ready[best] = send("y", size / 2)
        elif name == "a":
            ready[best] = send("y", size)
        elif name == "fin":
            ready[best] = send("z", size)
        elif name == "zf":
            ready[best] = send("z", size if step < hz - 2 else size / 2)
        span = SPANS.get({"fin": 0, "zf": step + 1, "xp": hz}.get(name))
        if span:
            last = send("x", (span[1] - span[0]) * size / 2)
            if name == "xp":
                ready[best] = last + 0.7
        at[best] += 1
    return order


def split3(value, first):
    high = value.astype(BF16)
    low = (value - high.astype(F32)).astype(BF16)
    return [high, high, low] if first else [high, low, high]


def kernel(ny, nz, chunks, *refs):
    (x_hbm, t_ref, perm_hbm, con_hbm, nui_hbm, pinv_hbm, col_hbm, out_ref), refs = refs[:8], refs[8:]
    (x_ref, perm_ref, con_ref, nui_ref, pinv_ref, req_ref, col_ref), refs = refs[:7], refs[7:]
    dsc, dcat, xcat, part, gpart, mts, gfin, mcol, tv, tcat, rq, rqs, eb, es = refs[:14]
    refs = refs[14:]
    sb, refs = refs[:chunks], refs[chunks:]
    rb, refs = refs[:chunks], refs[chunks:]
    zb, refs = [refs[c * nz : (c + 1) * nz] for c in range(chunks)], refs[chunks * nz :]
    pk, refs = refs[:chunks], refs[chunks:]
    xr, refs = refs[:chunks], refs[chunks:]
    er, yr, zr, xv, one, loc = refs
    hy, hz = ny // 2, nz // 2
    blocks = x_ref.shape[0] // BS
    half = blocks // 2
    rows = ROWS
    per_dest = rows * chunks
    perms = perm_ref.shape[0]
    regs = con_ref.shape[0]
    nuis = nui_ref.shape[0]
    cdim = perms * regs

    fix, y = lax.axis_index("fix"), lax.axis_index("subj")
    q = lax.rem(fix, NQ)
    x = lax.rem(fix // NQ, NX)
    z = fix // (NQ * NX)
    m = x * NQ + q

    def fix_of(zz, xx, qq):
        return (zz * NX + xx) * NQ + qq

    x_by = {0: x, 1: x + 1 - 2 * lax.rem(x, 2), 2: lax.rem(x + 2, NX), 3: NX - 1 - x}
    q_by = {0: q, 1: 1 - q}
    y_to = [lax.rem(y + 1, ny), lax.rem(y + ny - 1, ny)]
    z_to = [lax.rem(z + 1, nz), lax.rem(z + nz - 1, nz)]

    def y_dev(d):
        return (fix, y_to[d])

    def z_dev(d):
        return (fix_of(z_to[d], x, q), y)

    def x_dev(o):
        return (fix_of(z, x_by[o // 2], q_by[o % 2]), y)

    def x_slot(o):
        return x_by[o // 2] * NQ + q_by[o % 2]

    peers = [y_dev(0), y_dev(1), z_dev(0), z_dev(1)] + [x_dev(o) for o in range(1, 8)]
    barrier = pltpu.get_barrier_semaphore()
    for peer in peers:
        pl.semaphore_signal(barrier, inc=1, device_id=peer, device_id_type=MESH)

    loads = []
    for i, (src, dst) in enumerate((
        (perm_hbm, perm_ref), (con_hbm, con_ref), (x_hbm, x_ref), (nui_hbm, nui_ref),
        (pinv_hbm, pinv_ref), (col_hbm, col_ref), (t_ref, tv),
    )):
        loads.append(pltpu.make_async_copy(src, dst, loc.at[i]))
        if src is not t_ref:
            loads[-1].start()

    def arrived(ref, sem):
        pltpu.make_async_copy(ref, ref, sem).wait()

    def remote(src, dst, send_sem, recv_sem, device):
        copy = pltpu.make_async_remote_copy(
            src_ref=src, dst_ref=dst, send_sem=send_sem, recv_sem=recv_sem,
            device_id=device, device_id_type=MESH,
        )
        copy.start()

    loads[0].wait()
    loads[1].wait()
    index = perm_ref[...]
    group, lane = index // BS, lax.rem(index, BS)
    for r in range(regs):
        picked = jnp.zeros((perms, BS), F32)
        for g in range(con_ref.shape[1] // BS):
            table = jnp.broadcast_to(con_ref[r : r + 1, g * BS : (g + 1) * BS], (perms, BS))
            value = jnp.take_along_axis(table, lane, axis=1, mode="promise_in_bounds")
            picked = jnp.where(group == g, value, picked)
        dsc[pl.ds(r, perms, stride=regs), :] = picked
    for i, piece in enumerate(split3(dsc[...], True)):
        dcat[0:cdim, i * BS : (i + 1) * BS] = piece
    for i in range(2, 6):
        loads[i].wait()
    gap = jnp.zeros((EXTRA - nuis, BS), F32)
    pinv = jnp.concatenate([pinv_ref[...], gap, gap, pinv_ref[...]], axis=0)
    for i, piece in enumerate(split3(pinv, True)):
        dcat[cdim : cdim + 16, i * BS : (i + 1) * BS] = piece
    for i, piece in enumerate(split3(x_ref[...], False)):
        xcat[:, i * BS : (i + 1) * BS] = piece
    nui = jnp.concatenate([jnp.zeros((nuis, BS), F32), nui_ref[...], jnp.zeros((16 - 2 * nuis, BS), F32)], axis=0)
    ncat = jnp.concatenate(split3(nui, False), axis=1)
    load = lax.dot_general(ncat, dcat[0:cdim, :], NT, preferred_element_type=F32)
    for i in range(cdim // BS):
        mts[i] = load[0:EXTRA, i * BS : (i + 1) * BS]
    loads[6].start()
    far_dest = lax.rem(y + hy, ny)
    first = jnp.concatenate(
        [dcat[pl.ds(pl.multiple_of(far_dest * per_dest, per_dest), per_dest), :], dcat[cdim : cdim + 16, :]], axis=0)
    for b in range(0, blocks, 2):
        both = lax.dot_general(first, xcat[b * BS : (b + 2) * BS, :], NT, preferred_element_type=F32)
        for c in range(chunks):
            for i in range(2):
                sb[c][b + i] = both[c * rows : (c + 1) * rows, i * BS : (i + 1) * BS]
        gpart[b // 2] = both[per_dest : per_dest + EXTRA, 0:BS] + both[per_dest + EXTRA :, BS : 2 * BS]

    def store_own(ref, dest, c, lo, hi, add):
        top = part[dest, lo:hi, c * rows : (c + 1) * rows, :]
        ref[lo:hi, 0:rows, :] = ref[lo:hi, 0:rows, :] + top if add else top

    et = gpart.shape[0] + 1
    eh = et // 2
    per = BS // per_dest

    def store_extra(ref, dest, lo, hi, add):
        for i in range(lo, hi):
            value = gpart[i] if i < et - 1 else mts[dest // per]
            ref[i] = ref[i] + value if add else value

    line = lax.broadcasted_iota(jnp.int32, (nz, BS), 0)
    place = lax.broadcasted_iota(jnp.int32, (nz, BS), 1)
    place = jnp.where(place < NX * NQ, line * (NX * NQ) + place, -1)
    request = jnp.zeros((nz, BS), jnp.int32)
    for b in range(blocks):
        for k in range(tv.shape[1]):
            col = col_ref[k, b]
            request = jnp.where(place == col // blocks, lax.rem(col, blocks), request)
    req_ref[...] = request
    rq[m] = request

    pl.semaphore_wait(barrier, len(peers))

    def step_s0(c, _):
        out = one.at[4]
        if c == 0:
            store_extra(es, far_dest, 0, et, False)
            remote(es.at[0:eh], eb.at[0, 0:eh], one.at[5], er.at[0], y_dev(0))
            remote(es.at[eh:et], eb.at[1, eh:et], one.at[5], er.at[0], y_dev(1))
        remote(sb[c].at[0:half], rb[c].at[0, 0:half], out, yr.at[c, 0], y_dev(0))
        remote(sb[c].at[half:blocks], rb[c].at[1, half:blocks], out, yr.at[c, 0], y_dev(1))
        if c == 0:
            for o in range(1, 8):
                remote(req_ref, rq.at[m], one.at[2], one.at[3], x_dev(o))

    def dest_of(s, d):
        far = hy - 1 - s
        return lax.rem(y + (far if d == 0 else ny - far), ny)

    def step_a(c, s):
        if c == 0:
            arrived(eb.at[0] if s == 0 else eb.at[0:2], er.at[s % 2])
            for d in range(2):
                held = eb.at[2 * s + d]
                lo, hi = (0, et) if s else ((0, eh) if d == 0 else (eh, et))
                store_extra(held, dest_of(s, d), lo, hi, True)
                if s == 0:
                    store_extra(held, dest_of(s, d), hi % et, lo if lo else et, False)
                remote(held, eb.at[2 * s + 2 + d], one.at[5], er.at[(s + 1) % 2], y_dev(d))
        arrived(rb[c].at[0] if s == 0 else rb[c].at[0:2], yr.at[c, s % 2])
        for d in range(2):
            dest = dest_of(s, d)
            held = rb[c].at[2 * s + d]
            if s == 0:
                lo, hi = (0, half) if d == 0 else (half, blocks)
                store_own(held, dest, c, lo, hi, True)
                other = (half, blocks) if d == 0 else (0, half)
                store_own(held, dest, c, other[0], other[1], False)
            else:
                store_own(held, dest, c, 0, blocks, True)
            remote(held, rb[c].at[2 * s + 2 + d], one.at[4], yr.at[c, (s + 1) % 2], y_dev(d))

    def z_send(c, s, d):
        mine, theirs = ((nz - s) % nz, (nz - s - 1) % nz) if d == 0 else (s, s + 1)
        src, dst = zb[c][mine], zb[c][theirs]
        if s == hz - 1:
            lo, hi = (0, half) if d == 0 else (half, blocks)
            src, dst = src.at[lo:hi], dst.at[lo:hi]
        remote(src, dst, one.at[0], zr.at[c, s % 2], z_dev(d))

    slots = [0]
    for far in range(1, hz):
        slots += [far, nz - far]
    slots.append(hz)
    z_of = [lax.rem(z + slots[i], nz) for i in range(nz)]
    ready_asks = []

    def x_send(c, stage):
        if not ready_asks:
            arrived(rq.at[0:7], one.at[3])
            copy = pltpu.make_async_copy(rq, rqs, loc.at[7])
            copy.start()
            copy.wait()
            ready_asks.append(1)
        if stage not in SPANS:
            return
        lo, hi = SPANS[stage]
        for o in PARTNERS:
            e = x_slot(o)
            for i in range(lo, hi):
                pk[c][o, i] = zb[c][slots[i]][rqs[e, z_of[i], m]]
            remote(pk[c].at[o, lo:hi], xr[c].at[m, lo:hi], one.at[1], xv.at[c], x_dev(o))
        for i in range(lo, hi):
            xr[c][m, i] = zb[c][slots[i]][rqs[m, z_of[i], m]]

    def step_fin(c, _):
        arrived(rb[c].at[0:2], yr.at[c, (hy - 1) % 2])
        held = rb[c].at[2 * hy - 2]
        store_own(held, y, c, 0, blocks, True)
        if c == 0:
            arrived(eb.at[0:2], er.at[(hy - 1) % 2])
            last = eb.at[2 * hy - 2]
            store_extra(last, y, 0, et, True)
            for i in range(et - 1):
                more = last[i] + eb[2 * hy - 1, i]
                gfin[2 * i, 0:nuis, :] = more[0:nuis]
                gfin[2 * i + 1, 0:nuis, :] = more[nuis : 2 * nuis]
            square = jnp.concatenate(
                [last[et - 1] + eb[2 * hy - 1, et - 1], jnp.zeros((BS - EXTRA, BS), F32)], axis=0)
            mcol[...] = jnp.transpose(square)
        total = held[:, 0:rows, :] + rb[c][2 * hy - 1, :, 0:rows, :]
        cols = mcol[pl.ds(lax.rem(y, per) * per_dest + c * rows, rows), :]
        for n in range(nuis):
            weight = jnp.broadcast_to(cols[:, nuis + n : nuis + n + 1], (rows, BS))
            total = total - weight[None] * gfin[:, n : n + 1, :]
        zb[c][0][...] = total
        for d in range(2):
            z_send(c, 0, d)
        x_send(c, 0)

    def step_zf(c, s):
        arrived(part.at[0:2, :, 0:rows], zr.at[c, s % 2])
        for d in range(2):
            z_send(c, s + 1, d)
        x_send(c, s + 1)

    def step_xp(c, _):
        arrived(part.at[0:1, :, 0:rows], zr.at[c, (hz - 1) % 2])
        x_send(c, hz)

    def step_tp(b, _):
        if b == 0:
            loads[6].wait()
        for k in range(tv.shape[1]):
            tile = tv[b, k]
            high = tile.astype(BF16)
            tcat[b, 0:BS, k * BS : (k + 1) * BS] = high
            tcat[b, BS : 2 * BS, k * BS : (k + 1) * BS] = (tile - high.astype(F32)).astype(BF16)

    found = []

    def find():
        for b in range(blocks):
            for k in range(tv.shape[1]):
                owner = col_ref[k, b] // blocks
                far = lax.rem(owner // (NX * NQ) + nz - z, nz)
                slot = jnp.where(far < hz, jnp.maximum(2 * far - 1, 0), jnp.where(far == hz, nz - 1, 2 * (nz - far)))
                found.append((lax.rem(owner, NX * NQ), slot))

    def step_sm(c, _):
        if not found:
            find()
        arrived(xr[c].at[0:7], xv.at[c])
        for b in range(blocks):
            pieces = []
            for k in range(tv.shape[1]):
                who, slot = found[b * tv.shape[1] + k]
                pieces.append(xr[c][who, slot])
            value = jnp.concatenate(pieces, axis=1)
            high = value.astype(BF16).astype(F32)
            both = jnp.concatenate([high, value - high], axis=0).astype(BF16)
            got = lax.dot_general(both, tcat[b], NT, preferred_element_type=F32)
            out_ref[c * rows : (c + 1) * rows, b * BS : (b + 1) * BS] = got[0:rows, 0:BS] + (
                got[rows:, 0:BS] + got[0:rows, BS:] + got[rows:, BS:])

    steps = dict(s0=step_s0, a=step_a, fin=step_fin, zf=step_zf, xp=step_xp, tp=step_tp, sm=step_sm)
    for c in range(chunks):
        step_s0(c, 0)
    for b in range(0, blocks, 2):
        both = lax.dot_general(dcat[0:cdim, :], xcat[b * BS : (b + 2) * BS, :], NT, preferred_element_type=F32)
        for i in range(2):
            part[:, b + i] = both[:, i * BS : (i + 1) * BS].reshape(ny, per_dest, BS)
    for name, which, step in plan(chunks, hy, hz, blocks, rows):
        if name != "s0":
            steps[name](which, step)
    arrived(part.at[0 : 2 * hy - 1], one.at[4])
    arrived(eb.at[0 : 2 * hy - 1], one.at[5])
    arrived(part.at[0 : 2 * hz - 1], one.at[0])
    arrived(part.at[0:7], one.at[1])
    arrived(rq.at[0:7], one.at[2])


def per_device(fixels, conn_tiles, columns, nuisance, nuisance_pinv, contrast, perm_table):
    ny = lax.axis_size("subj")
    nz = lax.axis_size("fix") // (NX * NQ)
    blocks, tiles = columns.shape
    fixel_count = fixels.shape[0]
    perms, regs = perm_table.shape[0], contrast.shape[0]
    cdim = perms * regs
    per_dest = cdim // ny
    chunks = per_dest // ROWS
    group = NX * NQ
    vm = pltpu.VMEM
    rc = [ROWS] * chunks
    hy = ny // 2
    extra = blocks // 2 + 1
    sem = pltpu.SemaphoreType.DMA
    scratch = [
        vm(fixels.shape, F32), vm(perm_table.shape, jnp.int32), vm(contrast.shape, F32), vm(nuisance.shape, F32),
        vm(nuisance_pinv.shape, F32), vm((nz, BS), jnp.int32), pltpu.SMEM((tiles, blocks), jnp.int32),
        vm((cdim, BS), F32), vm((cdim + 16, 3 * BS), BF16), vm((fixel_count, 3 * BS), BF16),
        vm((ny, blocks, per_dest, BS), F32), vm((blocks // 2, EXTRA, BS), F32), vm((cdim // BS, EXTRA, BS), F32),
        vm((blocks, EXTRA, BS), F32), vm((BS, BS), F32),
        vm(conn_tiles.shape, F32), vm((blocks, 2 * BS, tiles * BS), BF16),
        vm((group, nz, BS), jnp.int32), pltpu.SMEM((group, nz, BS), jnp.int32),
        vm((2 * hy, extra, EXTRA, BS), F32), vm((extra, EXTRA, BS), F32),
    ]
    scratch += [vm((blocks, r, BS), F32) for r in rc]
    scratch += [vm((2 * hy, blocks, r, BS), F32) for r in rc]
    scratch += [vm((blocks, ROWS, BS), F32) for _ in rc for _ in range(nz)]
    scratch += [vm((group, nz, ROWS, BS), F32) for _ in rc]
    scratch += [vm((group, nz, ROWS, BS), F32) for _ in rc]
    scratch += [
        sem((2,)), sem((chunks, 2)), sem((chunks, 2)), sem((chunks,)), sem((6,)), sem((8,)),
    ]
    return pl.pallas_call(
        functools.partial(kernel, ny, nz, chunks),
        out_shape=jax.ShapeDtypeStruct((per_dest, fixel_count), F32),
        in_specs=[pl.BlockSpec(memory_space=pl.ANY)] * 7,
        out_specs=pl.BlockSpec(memory_space=pltpu.VMEM),
        scratch_shapes=scratch,
        compiler_params=pltpu.CompilerParams(collective_id=0, has_side_effects=True),
        name="project_exchange",
    )(fixels, conn_tiles, perm_table, contrast, nuisance, nuisance_pinv, columns.T)


def solution(mesh):
    placed = (
        P("fix", "subj"),
        P("fix", None, None, None),
        P("fix", None),
        P(None, "subj"),
        P(None, "subj"),
        P(),
        P(None, "subj"),
    )
    return jax.shard_map(
        per_device, mesh=mesh, in_specs=placed, out_specs=P("subj", "fix"), check_vma=False
    )
```

```python
import functools

import jax
import jax.numpy as jnp
from jax import lax
from jax.experimental import pallas as pl
from jax.experimental.pallas import tpu as pltpu
from jax.sharding import PartitionSpec as P

MESH = pl.DeviceIdType.MESH
F32, BF16 = jnp.float32, jnp.bfloat16
BS = 128
NX, NQ = 4, 2
ROWS = 16
WINDOW = 4
RATE, LATENCY, GAP, SLACK = 50e3, 2.9, 0.1, 0.8
SPANS = {0: (0, 1), 1: (1, 3), 2: (3, 5), 3: (5, 7), 4: (7, 8)}
EXTRA = 8
NT = (((1,), (1,)), ((), ()))
PARTNERS = (4, 5, 2, 3, 6, 7, 1)


def plan(chunks, hy, hz, tiles, rows):
    size = rows * BS * 4 * 8
    cost = dict(s0=0.1, a=0.1, fin=0.3, zf=0.2, xp=0.1, sm=0.8, tp=0.25)
    stages = [("s0", 0)] + [("a", s) for s in range(hy - 1)] + [("fin", 0)]
    stages += [("zf", s) for s in range(hz - 1)] + [("xp", 0), ("sm", 0)]
    wire = dict(s0="y", a="y", fin="z", zf="z")
    free = dict(y=0.0, z=0.0, x=0.0)
    at, ready = [0] * chunks, [0.0] * chunks
    order, t, prepared = [], 0.0, 0

    def send(link, amount):
        free[link] = max(free[link], t) + amount / RATE + GAP
        return free[link] + LATENCY

    while any(i < len(stages) for i in at):
        best, late, soonest = None, None, 1e9
        for c in range(chunks):
            if at[c] == len(stages):
                continue
            name, when = stages[at[c]][0], ready[c]
            if name == "s0" and c and at[c - 1] == 0:
                continue
            if name == "s0" and sum(0 < i <= hy for i in at) >= WINDOW:
                continue
            if name in wire:
                when = max(when, free[wire[name]] - SLACK)
            if name == "sm":
                if prepared < tiles:
                    continue
                if when <= t and late is None:
                    late = c
            elif when <= t and best is None:
                best = c
            soonest = min(soonest, when)
        best = late if best is None else best
        if best is None:
            if prepared < tiles and order:
                order.append(("tp", prepared, 0))
                prepared += 1
                t += cost["tp"]
            else:
                t = max(soonest, t + 1e-6)
            continue
        name, step = stages[at[best]]
        order.append((name, best, step))
        t += cost[name]
        if name == "s0":
            ready[best] = send("y", size / 2)
        elif name == "a":
            ready[best] = send("y", size)
        elif name == "fin":
            ready[best] = send("z", size)
        elif name == "zf":
            ready[best] = send("z", size if step < hz - 2 else size / 2)
        span = SPANS.get({"fin": 0, "zf": step + 1, "xp": hz}.get(name))
        if span:
            last = send("x", (span[1] - span[0]) * size / 2)
            if name == "xp":
                ready[best] = last + 0.7
        at[best] += 1
    return order


def split3(value, first):
    high = value.astype(BF16)
    low = (value - high.astype(F32)).astype(BF16)
    return [high, high, low] if first else [high, low, high]


def kernel(ny, nz, chunks, *refs):
    (x_hbm, t_ref, perm_hbm, con_hbm, nui_hbm, pinv_hbm, col_hbm, out_ref), refs = refs[:8], refs[8:]
    (x_ref, perm_ref, con_ref, nui_ref, pinv_ref, req_ref, col_ref), refs = refs[:7], refs[7:]
    dsc, dcat, xcat, part, gpart, mts, gfin, mcol, tv, tcat, rq, rqs, eb, es = refs[:14]
    refs = refs[14:]
    sb, refs = refs[:chunks], refs[chunks:]
    rb, refs = refs[:chunks], refs[chunks:]
    zb, refs = [refs[c * nz : (c + 1) * nz] for c in range(chunks)], refs[chunks * nz :]
    pk, refs = refs[:chunks], refs[chunks:]
    xr, refs = refs[:chunks], refs[chunks:]
    er, yr, zr, xv, one, loc = refs
    hy, hz = ny // 2, nz // 2
    blocks = x_ref.shape[0] // BS
    half = blocks // 2
    rows = ROWS
    per_dest = rows * chunks
    perms = perm_ref.shape[0]
    regs = con_ref.shape[0]
    nuis = nui_ref.shape[0]
    cdim = perms * regs

    fix, y = lax.axis_index("fix"), lax.axis_index("subj")
    q = lax.rem(fix, NQ)
    x = lax.rem(fix // NQ, NX)
    z = fix // (NQ * NX)
    m = x * NQ + q

    def fix_of(zz, xx, qq):
        return (zz * NX + xx) * NQ + qq

    x_by = {0: x, 1: x + 1 - 2 * lax.rem(x, 2), 2: lax.rem(x + 2, NX), 3: NX - 1 - x}
    q_by = {0: q, 1: 1 - q}
    y_to = [lax.rem(y + 1, ny), lax.rem(y + ny - 1, ny)]
    z_to = [lax.rem(z + 1, nz), lax.rem(z + nz - 1, nz)]

    def y_dev(d):
        return (fix, y_to[d])

    def z_dev(d):
        return (fix_of(z_to[d], x, q), y)

    def x_dev(o):
        return (fix_of(z, x_by[o // 2], q_by[o % 2]), y)

    def x_slot(o):
        return x_by[o // 2] * NQ + q_by[o % 2]

    peers = [y_dev(0), y_dev(1), z_dev(0), z_dev(1)] + [x_dev(o) for o in range(1, 8)]
    barrier = pltpu.get_barrier_semaphore()
    for peer in peers:
        pl.semaphore_signal(barrier, inc=1, device_id=peer, device_id_type=MESH)

    loads = []
    for i, (src, dst) in enumerate((
        (perm_hbm, perm_ref), (con_hbm, con_ref), (x_hbm, x_ref), (nui_hbm, nui_ref),
        (pinv_hbm, pinv_ref), (col_hbm, col_ref), (t_ref, tv),
    )):
        loads.append(pltpu.make_async_copy(src, dst, loc.at[i]))
        loads[-1].start()

    def arrived(ref, sem):
        pltpu.make_async_copy(ref, ref, sem).wait()

    def remote(src, dst, send_sem, recv_sem, device):
        copy = pltpu.make_async_remote_copy(
            src_ref=src, dst_ref=dst, send_sem=send_sem, recv_sem=recv_sem,
            device_id=device, device_id_type=MESH,
        )
        copy.start()

    loads[0].wait()
    loads[1].wait()
    index = perm_ref[...]
    group, lane = index // BS, lax.rem(index, BS)
    for r in range(regs):
        picked = jnp.zeros((perms, BS), F32)
        for g in range(con_ref.shape[1] // BS):
            table = jnp.broadcast_to(con_ref[r : r + 1, g * BS : (g + 1) * BS], (perms, BS))
            value = jnp.take_along_axis(table, lane, axis=1, mode="promise_in_bounds")
            picked = jnp.where(group == g, value, picked)
        dsc[pl.ds(r, perms, stride=regs), :] = picked
    for i, piece in enumerate(split3(dsc[...], True)):
        dcat[0:cdim, i * BS : (i + 1) * BS] = piece
    for i in range(2, 6):
        loads[i].wait()
    gap = jnp.zeros((EXTRA - nuis, BS), F32)
    pinv = jnp.concatenate([pinv_ref[...], gap, gap, pinv_ref[...]], axis=0)
    for i, piece in enumerate(split3(pinv, True)):
        dcat[cdim : cdim + 16, i * BS : (i + 1) * BS] = piece
    for i, piece in enumerate(split3(x_ref[...], False)):
        xcat[:, i * BS : (i + 1) * BS] = piece
    nui = jnp.concatenate([jnp.zeros((nuis, BS), F32), nui_ref[...], jnp.zeros((16 - 2 * nuis, BS), F32)], axis=0)
    ncat = jnp.concatenate(split3(nui, False), axis=1)
    load = lax.dot_general(ncat, dcat[0:cdim, :], NT, preferred_element_type=F32)
    for i in range(cdim // BS):
        mts[i] = load[0:EXTRA, i * BS : (i + 1) * BS]
    far_dest = lax.rem(y + hy, ny)
    first = jnp.concatenate(
        [dcat[pl.ds(pl.multiple_of(far_dest * per_dest, per_dest), per_dest), :], dcat[cdim : cdim + 16, :]], axis=0)
    for b in range(0, blocks, 2):
        both = lax.dot_general(first, xcat[b * BS : (b + 2) * BS, :], NT, preferred_element_type=F32)
        for c in range(chunks):
            for i in range(2):
                sb[c][b + i] = both[c * rows : (c + 1) * rows, i * BS : (i + 1) * BS]
        gpart[b // 2] = both[per_dest : per_dest + EXTRA, 0:BS] + both[per_dest + EXTRA :, BS : 2 * BS]

    def store_own(ref, dest, c, lo, hi, add):
        top = part[dest, lo:hi, c * rows : (c + 1) * rows, :]
        ref[lo:hi, 0:rows, :] = ref[lo:hi, 0:rows, :] + top if add else top

    et = gpart.shape[0] + 1
    eh = et // 2
    per = BS // per_dest

    def store_extra(ref, dest, lo, hi, add):
        for i in range(lo, hi):
            value = gpart[i] if i < et - 1 else mts[dest // per]
            ref[i] = ref[i] + value if add else value

    line = lax.broadcasted_iota(jnp.int32, (nz, BS), 0)
    place = lax.broadcasted_iota(jnp.int32, (nz, BS), 1)
    place = jnp.where(place < NX * NQ, line * (NX * NQ) + place, -1)
    request = jnp.zeros((nz, BS), jnp.int32)
    for b in range(blocks):
        for k in range(tv.shape[1]):
            col = col_ref[k, b]
            request = jnp.where(place == col // blocks, lax.rem(col, blocks), request)
    req_ref[...] = request
    rq[m] = request

    pl.semaphore_wait(barrier, len(peers))

    def step_s0(c, _):
        out = one.at[4]
        if c == 0:
            store_extra(es, far_dest, 0, et, False)
            remote(es.at[0:eh], eb.at[0, 0:eh], one.at[5], er.at[0], y_dev(0))
            remote(es.at[eh:et], eb.at[1, eh:et], one.at[5], er.at[0], y_dev(1))
        remote(sb[c].at[0:half], rb[c].at[0, 0:half], out, yr.at[c, 0], y_dev(0))
        remote(sb[c].at[half:blocks], rb[c].at[1, half:blocks], out, yr.at[c, 0], y_dev(1))
        if c == 0:
            for o in range(1, 8):
                remote(req_ref, rq.at[m], one.at[2], one.at[3], x_dev(o))

    def dest_of(s, d):
        far = hy - 1 - s
        return lax.rem(y + (far if d == 0 else ny - far), ny)

    def step_a(c, s):
        if c == 0:
            arrived(eb.at[0] if s == 0 else eb.at[0:2], er.at[s % 2])
            for d in range(2):
                held = eb.at[2 * s + d]
                lo, hi = (0, et) if s else ((0, eh) if d == 0 else (eh, et))
                store_extra(held, dest_of(s, d), lo, hi, True)
                if s == 0:
                    store_extra(held, dest_of(s, d), hi % et, lo if lo else et, False)
                remote(held, eb.at[2 * s + 2 + d], one.at[5], er.at[(s + 1) % 2], y_dev(d))
        arrived(rb[c].at[0] if s == 0 else rb[c].at[0:2], yr.at[c, s % 2])
        for d in range(2):
            dest = dest_of(s, d)
            held = rb[c].at[2 * s + d]
            if s == 0:
                lo, hi = (0, half) if d == 0 else (half, blocks)
                store_own(held, dest, c, lo, hi, True)
                other = (half, blocks) if d == 0 else (0, half)
                store_own(held, dest, c, other[0], other[1], False)
            else:
                store_own(held, dest, c, 0, blocks, True)
            remote(held, rb[c].at[2 * s + 2 + d], one.at[4], yr.at[c, (s + 1) % 2], y_dev(d))

    def z_send(c, s, d):
        mine, theirs = ((nz - s) % nz, (nz - s - 1) % nz) if d == 0 else (s, s + 1)
        src, dst = zb[c][mine], zb[c][theirs]
        if s == hz - 1:
            lo, hi = (0, half) if d == 0 else (half, blocks)
            src, dst = src.at[lo:hi], dst.at[lo:hi]
        remote(src, dst, one.at[0], zr.at[c, s % 2], z_dev(d))

    slots = [0]
    for far in range(1, hz):
        slots += [far, nz - far]
    slots.append(hz)
    z_of = [lax.rem(z + slots[i], nz) for i in range(nz)]
    ready_asks = []

    def x_send(c, stage):
        if not ready_asks:
            arrived(rq.at[0:7], one.at[3])
            copy = pltpu.make_async_copy(rq, rqs, loc.at[7])
            copy.start()
            copy.wait()
            ready_asks.append(1)
        if stage not in SPANS:
            return
        lo, hi = SPANS[stage]
        for o in PARTNERS:
            e = x_slot(o)
            for i in range(lo, hi):
                pk[c][o, i] = zb[c][slots[i]][rqs[e, z_of[i], m]]
            remote(pk[c].at[o, lo:hi], xr[c].at[m, lo:hi], one.at[1], xv.at[c], x_dev(o))
        for i in range(lo, hi):
            xr[c][m, i] = zb[c][slots[i]][rqs[m, z_of[i], m]]

    def step_fin(c, _):
        arrived(rb[c].at[0:2], yr.at[c, (hy - 1) % 2])
        held = rb[c].at[2 * hy - 2]
        store_own(held, y, c, 0, blocks, True)
        if c == 0:
            arrived(eb.at[0:2], er.at[(hy - 1) % 2])
            last = eb.at[2 * hy - 2]
            store_extra(last, y, 0, et, True)
            for i in range(et - 1):
                more = last[i] + eb[2 * hy - 1, i]
                gfin[2 * i, 0:nuis, :] = more[0:nuis]
                gfin[2 * i + 1, 0:nuis, :] = more[nuis : 2 * nuis]
            square = jnp.concatenate(
                [last[et - 1] + eb[2 * hy - 1, et - 1], jnp.zeros((BS - EXTRA, BS), F32)], axis=0)
            mcol[...] = jnp.transpose(square)
        total = held[:, 0:rows, :] + rb[c][2 * hy - 1, :, 0:rows, :]
        cols = mcol[pl.ds(lax.rem(y, per) * per_dest + c * rows, rows), :]
        for n in range(nuis):
            weight = jnp.broadcast_to(cols[:, nuis + n : nuis + n + 1], (rows, BS))
            total = total - weight[None] * gfin[:, n : n + 1, :]
        zb[c][0][...] = total
        for d in range(2):
            z_send(c, 0, d)
        x_send(c, 0)

    def step_zf(c, s):
        arrived(part.at[0:2, :, 0:rows], zr.at[c, s % 2])
        for d in range(2):
            z_send(c, s + 1, d)
        x_send(c, s + 1)

    def step_xp(c, _):
        arrived(part.at[0:1, :, 0:rows], zr.at[c, (hz - 1) % 2])
        x_send(c, hz)

    def step_tp(b, _):
        if b == 0:
            loads[6].wait()
        for k in range(tv.shape[1]):
            tile = tv[b, k]
            high = tile.astype(BF16)
            tcat[b, 0:BS, k * BS : (k + 1) * BS] = high
            tcat[b, BS : 2 * BS, k * BS : (k + 1) * BS] = (tile - high.astype(F32)).astype(BF16)

    found = []

    def find():
        for b in range(blocks):
            for k in range(tv.shape[1]):
                owner = col_ref[k, b] // blocks
                far = lax.rem(owner // (NX * NQ) + nz - z, nz)
                slot = jnp.where(far < hz, jnp.maximum(2 * far - 1, 0), jnp.where(far == hz, nz - 1, 2 * (nz - far)))
                found.append((lax.rem(owner, NX * NQ), slot))

    def step_sm(c, _):
        if not found:
            find()
        arrived(xr[c].at[0:7], xv.at[c])
        for b in range(blocks):
            pieces = []
            for k in range(tv.shape[1]):
                who, slot = found[b * tv.shape[1] + k]
                pieces.append(xr[c][who, slot])
            value = jnp.concatenate(pieces, axis=1)
            high = value.astype(BF16).astype(F32)
            both = jnp.concatenate([high, value - high], axis=0).astype(BF16)
            got = lax.dot_general(both, tcat[b], NT, preferred_element_type=F32)
            out_ref[c * rows : (c + 1) * rows, b * BS : (b + 1) * BS] = got[0:rows, 0:BS] + (
                got[rows:, 0:BS] + got[0:rows, BS:] + got[rows:, BS:])

    steps = dict(s0=step_s0, a=step_a, fin=step_fin, zf=step_zf, xp=step_xp, tp=step_tp, sm=step_sm)
    for c in range(chunks):
        step_s0(c, 0)
    for b in range(0, blocks, 2):
        both = lax.dot_general(dcat[0:cdim, :], xcat[b * BS : (b + 2) * BS, :], NT, preferred_element_type=F32)
        for i in range(2):
            part[:, b + i] = both[:, i * BS : (i + 1) * BS].reshape(ny, per_dest, BS)
    for name, which, step in plan(chunks, hy, hz, blocks, rows):
        if name != "s0":
            steps[name](which, step)
    arrived(part.at[0 : 2 * hy - 1], one.at[4])
    arrived(eb.at[0 : 2 * hy - 1], one.at[5])
    arrived(part.at[0 : 2 * hz - 1], one.at[0])
    arrived(part.at[0:7], one.at[1])
    arrived(rq.at[0:7], one.at[2])


def write_out(held, out, done):
    part = held.shape[0] // 4
    copies = []
    for i in range(4):
        copies.append(pltpu.make_async_copy(
            held.at[i * part : (i + 1) * part], out.at[i * part : (i + 1) * part], done.at[i]))
        copies[-1].start()
    for copy in copies:
        copy.wait()


def per_device(fixels, conn_tiles, columns, nuisance, nuisance_pinv, contrast, perm_table):
    ny = lax.axis_size("subj")
    nz = lax.axis_size("fix") // (NX * NQ)
    blocks, tiles = columns.shape
    fixel_count = fixels.shape[0]
    perms, regs = perm_table.shape[0], contrast.shape[0]
    cdim = perms * regs
    per_dest = cdim // ny
    chunks = per_dest // ROWS
    group = NX * NQ
    vm = pltpu.VMEM
    rc = [ROWS] * chunks
    hy = ny // 2
    extra = blocks // 2 + 1
    sem = pltpu.SemaphoreType.DMA
    scratch = [
        vm(fixels.shape, F32), vm(perm_table.shape, jnp.int32), vm(contrast.shape, F32), vm(nuisance.shape, F32),
        vm(nuisance_pinv.shape, F32), vm((nz, BS), jnp.int32), pltpu.SMEM((tiles, blocks), jnp.int32),
        vm((cdim, BS), F32), vm((cdim + 16, 3 * BS), BF16), vm((fixel_count, 3 * BS), BF16),
        vm((ny, blocks, per_dest, BS), F32), vm((blocks // 2, EXTRA, BS), F32), vm((cdim // BS, EXTRA, BS), F32),
        vm((blocks, EXTRA, BS), F32), vm((BS, BS), F32),
        vm(conn_tiles.shape, F32), vm((blocks, 2 * BS, tiles * BS), BF16),
        vm((group, nz, BS), jnp.int32), pltpu.SMEM((group, nz, BS), jnp.int32),
        vm((2 * hy, extra, EXTRA, BS), F32), vm((extra, EXTRA, BS), F32),
    ]
    scratch += [vm((blocks, r, BS), F32) for r in rc]
    scratch += [vm((2 * hy, blocks, r, BS), F32) for r in rc]
    scratch += [vm((blocks, ROWS, BS), F32) for _ in rc for _ in range(nz)]
    scratch += [vm((group, nz, ROWS, BS), F32) for _ in rc]
    scratch += [vm((group, nz, ROWS, BS), F32) for _ in rc]
    scratch += [
        sem((2,)), sem((chunks, 2)), sem((chunks, 2)), sem((chunks,)), sem((6,)), sem((8,)),
    ]
    held = pl.pallas_call(
        functools.partial(kernel, ny, nz, chunks),
        out_shape=jax.ShapeDtypeStruct((per_dest, fixel_count), F32),
        in_specs=[pl.BlockSpec(memory_space=pl.ANY)] * 7,
        out_specs=pl.BlockSpec(memory_space=pltpu.VMEM),
        scratch_shapes=scratch,
        compiler_params=pltpu.CompilerParams(collective_id=0, has_side_effects=True),
        name="project_exchange",
    )(fixels, conn_tiles, perm_table, contrast, nuisance, nuisance_pinv, columns.T)
    return pl.pallas_call(
        write_out,
        out_shape=jax.ShapeDtypeStruct((per_dest, fixel_count), F32),
        in_specs=[pl.BlockSpec(memory_space=pltpu.VMEM)],
        out_specs=pl.BlockSpec(memory_space=pl.ANY),
        scratch_shapes=[sem((4,))],
        name="write_out",
    )(held)


def solution(mesh):
    placed = (
        P("fix", "subj"),
        P("fix", None, None, None),
        P("fix", None),
        P(None, "subj"),
        P(None, "subj"),
        P(),
        P(None, "subj"),
    )
    return jax.shard_map(
        per_device, mesh=mesh, in_specs=placed, out_specs=P("subj", "fix"), check_vma=False
    )
```
